32 devices in a mesh: dp: 8 (over z, y), tm: 4 (over x, core).
Axes of the slice: x: 2, y: 2, z: 4, core: 2. Of those that a mesh axis runs over, the one named last changes fastest.
Arguments:
- inputs: bfloat16 [8, 4096, 512], P('dp', 'tm'), may hold values from -6 to 6
- w_query: bfloat16 [512, 512], replicated, may hold values from -0.25 to 0.25
- w_key: bfloat16 [512, 512], replicated, may hold values from -0.25 to 0.25
- w_value: bfloat16 [512, 512], replicated, may hold values from -0.25 to 0.25
- w_out: bfloat16 [512, 512], replicated, may hold values from -0.25 to 0.25
- saved_heads: bfloat16 [8, 4096, 512], P('dp', 'tm'), may hold values from -6 to 6
- log_totals: float32 [8, 8, 4096], P('dp', None, 'tm'), may hold values from 0 to 8
- out_grad: bfloat16 [8, 4096, 512], P('dp', 'tm'), may hold values from -6 to 6
Outputs:
- input_grad: bfloat16 [8, 4096, 512], P('dp', 'tm')
- weight_grads: float32 [2048, 512], P(('dp', 'tm'))
The draws below stay inside these ranges and needn't reach their ends.
All inputs are finite; a program needn't handle non-finite values.
Results may differ from the reference program's by a relative error of at most 0.012.
Values may be sent and summed in bfloat16 or wider, within the bound.
No kernel may reach another device: no remote copies, remote signals or barrier semaphores. Data moves between devices by JAX's collectives and lax.ppermute only.
A program may use at most 128 MiB of HBM per device.

```python
import jax
import jax.numpy as jnp
from jax import lax

WIDTH = 512
HEADS = 8
HEAD_DIM = 64
WINDOW = 1024
SHARD_BINS = 1024
QUERY_BLOCK = 512
RECORDINGS = 8
BINS = 4096


def draw_inputs(key, part):
    values = jax.random.truncated_normal(key, -6.0, 6.0, (RECORDINGS, BINS, WIDTH), jnp.float32)
    return values.astype(jnp.bfloat16)


def draw_log_totals(key, part):
    positions = jnp.arange(BINS, dtype=jnp.float32)
    counts = jnp.minimum(positions + 1.0, float(WINDOW))
    noise = jax.random.uniform(key, (RECORDINGS, HEADS, BINS), jnp.float32, -0.4, 0.4)
    return jnp.log(counts)[None, None, :] + 0.5 + noise


def spiked(array, stream_key, source, target, parts, factor):
    def block_of(dim):
        return (jnp.arange(array.shape[dim]) // (array.shape[dim] // parts)).reshape((-1,) + (1,) * (array.ndim - 1 - dim))

    near = jax.random.permutation(stream_key, parts)[block_of(target)]
    far = (block_of(target) + parts // 2) % parts
    return jnp.where((block_of(source) == near) | (block_of(source) == far), factor * array, array)


def level_of(key, dims, shards, least, top_value):
    factor_of, own = 1.0, jax.random.fold_in(key, 6)
    for dim, shards_of in shards:
        heights = jnp.exp(jax.random.uniform(jax.random.fold_in(own, dim), (shards_of,), jnp.float32, least / len(shards), top_value / len(shards)))
        factor_of = factor_of * jnp.repeat(heights, dims[dim] // shards_of).reshape([-1 if axis == dim else 1 for axis in range(len(dims))])
    return factor_of


def centred(key, shape, deviation, limit, shards=(), held_as=jnp.bfloat16):
    entries = deviation * jax.random.normal(key, shape, jnp.float32)
    if shards:
        entries = entries * level_of(key, shape, shards, -0.22, 0.18)
    return jnp.clip(entries, -limit, limit).astype(held_as)


def gaussian_with(stream_key, dims, deviation, reach, pieces, heavy, kind=jnp.bfloat16):
    values = deviation * jax.random.normal(stream_key, dims, jnp.float32)
    if pieces:
        values = values * level_of(stream_key, dims, pieces, -0.22, 0.18)
    return jnp.clip(spiked(values, jax.random.fold_in(stream_key, 3), *heavy), -reach, reach).astype(kind)


def setup_inputs(seed: int = 0) -> dict:
    seeds = jax.random.split(jax.random.key(seed), 9)
    return {
        "inputs": draw_inputs(jax.random.fold_in(seeds[8], 71), 0),
        "w_query": centred(seeds[1], (WIDTH, WIDTH), WIDTH ** -0.5, 0.25),
        "w_key": centred(seeds[2], (WIDTH, WIDTH), WIDTH ** -0.5, 0.25),
        "w_value": centred(seeds[3], (WIDTH, WIDTH), WIDTH ** -0.5, 0.25),
        "w_out": centred(seeds[4], (WIDTH, WIDTH), WIDTH ** -0.5, 0.25),
        "saved_heads": gaussian_with(seeds[5], (RECORDINGS, BINS, WIDTH), 1.0, 6.0, ((0, 8), (1, 4)), (1, 2, 4, 2.0)),
        "log_totals": draw_log_totals(jax.random.fold_in(seeds[8], 71), 0),
        "out_grad": centred(seeds[7], (RECORDINGS, BINS, WIDTH), 1.0, 6.0, ((0, 8), (1, 4))),
    }


def split_heads(matrix):
    return matrix.reshape(matrix.shape[0], HEADS, HEAD_DIM).transpose(1, 0, 2)


def join_heads(tensor):
    return tensor.transpose(1, 0, 2).reshape(tensor.shape[1], HEADS * HEAD_DIM)


def block_grads(query_heads, key_heads, value_heads, grad_heads, saved_split, total_rows, allowed):
    score_scale = HEAD_DIM ** -0.5

    def per_head(head_items):
        query_rows, key_rows, value_rows, grad_rows, saved_rows, lse_rows = head_items
        scores = jnp.dot(query_rows, key_rows.T, preferred_element_type=jnp.float32) * score_scale
        soft_weights = jnp.where(allowed, jnp.exp(scores - lse_rows[:, None]), 0.0)
        weights_low = soft_weights.astype(jnp.bfloat16)
        offsets = jnp.sum(grad_rows.astype(jnp.float32) * saved_rows.astype(jnp.float32), axis=1)
        prob_grad = jnp.dot(grad_rows, value_rows.T, preferred_element_type=jnp.float32)
        score_grad = (soft_weights * (prob_grad - offsets[:, None]) * score_scale).astype(jnp.bfloat16)
        grad_query = jnp.dot(score_grad, key_rows, preferred_element_type=jnp.float32)
        grad_key = jnp.dot(score_grad.T, query_rows, preferred_element_type=jnp.float32)
        grad_value = jnp.dot(weights_low.T, grad_rows, preferred_element_type=jnp.float32)
        return grad_query, grad_key, grad_value

    return lax.map(per_head, (query_heads, key_heads, value_heads, grad_heads, saved_split, total_rows))


def reference(inputs, w_query, w_key, w_value, w_out, saved_heads, log_totals, out_grad):
    bins_all = inputs.shape[1]
    row_ids = jnp.arange(QUERY_BLOCK, dtype=jnp.int32)[:, None]
    col_ids = jnp.arange(QUERY_BLOCK + WINDOW, dtype=jnp.int32)[None, :]

    def per_recording(rec_items):
        signal, saved, totals, upstream = rec_items
        query_full = jnp.dot(signal, w_query, preferred_element_type=jnp.float32).astype(jnp.bfloat16)
        key_full = jnp.dot(signal, w_key, preferred_element_type=jnp.float32).astype(jnp.bfloat16)
        value_full = jnp.dot(signal, w_value, preferred_element_type=jnp.float32).astype(jnp.bfloat16)
        head_grad = jnp.dot(upstream, w_out.T, preferred_element_type=jnp.float32).astype(jnp.bfloat16)
        grad_out_weight = jnp.dot(saved.T, upstream, preferred_element_type=jnp.float32)
        query_heads = split_heads(query_full)
        padding = jnp.zeros((HEADS, WINDOW, HEAD_DIM), jnp.bfloat16)
        key_padded = jnp.concatenate([padding, split_heads(key_full)], axis=1)
        value_padded = jnp.concatenate([padding, split_heads(value_full)], axis=1)
        grad_split = split_heads(head_grad)
        saved_split = split_heads(saved)

        def step(carry, block):
            key_near, key_far, value_near, value_far = carry
            start = (block * QUERY_BLOCK).astype(jnp.int32)
            query_block = lax.dynamic_slice_in_dim(query_heads, start, QUERY_BLOCK, 1)
            grad_block = lax.dynamic_slice_in_dim(grad_split, start, QUERY_BLOCK, 1)
            saved_block = lax.dynamic_slice_in_dim(saved_split, start, QUERY_BLOCK, 1)
            total_block = lax.dynamic_slice_in_dim(totals, start, QUERY_BLOCK, 1)
            key_block = lax.dynamic_slice_in_dim(key_padded, start, QUERY_BLOCK + WINDOW, 1)
            value_block = lax.dynamic_slice_in_dim(value_padded, start, QUERY_BLOCK + WINDOW, 1)
            query_pos = start + row_ids
            key_pos = start - WINDOW + col_ids
            allowed = (key_pos <= query_pos) & (key_pos > query_pos - WINDOW) & (key_pos >= 0)
            grad_query, grad_key, grad_value = block_grads(query_block, key_block, value_block, grad_block, saved_block, total_block, allowed)
            shard_begin = (start // SHARD_BINS) * SHARD_BINS
            near_mask = (key_pos[0] >= shard_begin).astype(jnp.float32)[None, :, None]
            far_mask = 1.0 - near_mask
            out = []
            for acc, term, mask in ((key_near, grad_key, near_mask), (key_far, grad_key, far_mask),
                                    (value_near, grad_value, near_mask), (value_far, grad_value, far_mask)):
                old = lax.dynamic_slice_in_dim(acc, start, QUERY_BLOCK + WINDOW, 1)
                out.append(lax.dynamic_update_slice_in_dim(acc, old + term * mask, start, 1))
            return tuple(out), grad_query

        zero_acc = jnp.zeros((HEADS, bins_all + WINDOW, HEAD_DIM), jnp.float32)
        blocks = jnp.arange(bins_all // QUERY_BLOCK, dtype=jnp.int32)
        accs, query_grads = lax.scan(step, (zero_acc, zero_acc, zero_acc, zero_acc), blocks)
        query_grad_heads = query_grads.transpose(1, 0, 2, 3).reshape(HEADS, bins_all, HEAD_DIM)
        grad_query_full = join_heads(query_grad_heads).astype(jnp.bfloat16)
        key_near, key_far, value_near, value_far = [join_heads(acc[:, WINDOW:]).astype(jnp.bfloat16) for acc in accs]
        input_grad = (jnp.dot(grad_query_full, w_query.T, preferred_element_type=jnp.float32)
                      + jnp.dot(key_near, w_key.T, preferred_element_type=jnp.float32)
                      + jnp.dot(key_far, w_key.T, preferred_element_type=jnp.float32)
                      + jnp.dot(value_near, w_value.T, preferred_element_type=jnp.float32)
                      + jnp.dot(value_far, w_value.T, preferred_element_type=jnp.float32)).astype(jnp.bfloat16)
        weight_grads = jnp.concatenate([
            jnp.dot(signal.T, grad_query_full, preferred_element_type=jnp.float32),
            jnp.dot(signal.T, key_near, preferred_element_type=jnp.float32)
            + jnp.dot(signal.T, key_far, preferred_element_type=jnp.float32),
            jnp.dot(signal.T, value_near, preferred_element_type=jnp.float32)
            + jnp.dot(signal.T, value_far, preferred_element_type=jnp.float32),
            grad_out_weight], axis=0)
        return input_grad, weight_grads

    input_grad, weight_grads = lax.map(per_recording, (inputs, saved_heads, log_totals, out_grad))
    return input_grad, jnp.sum(weight_grads, axis=0)
```

```python
import functools
import math

import jax
import jax.numpy as jnp
from jax import lax
from jax.experimental import pallas as pl
from jax.experimental.pallas import tpu as pltpu
from jax.sharding import PartitionSpec as P

HEADS = 8
HEAD_DIM = 64
TILE = 256
SCALE = HEAD_DIM**-0.5
LOG2E = math.log2(math.e)
LN2 = math.log(2.0)
F32 = jnp.float32
BF16 = jnp.bfloat16
VMEM = pl.BlockSpec(memory_space=pltpu.VMEM)


def mm(a, b, ca, cb):
    return lax.dot_general(a, b, (((ca,), (cb,)), ((), ())), preferred_element_type=F32)


def twice(x):
    return jnp.concatenate([x, x], axis=1)


def half_mask(h):
    lane = lax.broadcasted_iota(jnp.int32, (1, 128), 1)
    return lane < HEAD_DIM if h == 0 else lane >= HEAD_DIM


def attention(near, refs, scratch, put_query, put_key, put_value):
    q_ref, do_ref, qt_ref, dot_ref, k_ref, v_ref, aux_ref = refs
    km, vm, lseb, offb, prob, grad, acc = scratch
    bins = q_ref.shape[0]
    blocks = bins // TILE

    def body(pair, carry):
        base = pl.multiple_of(pair * 128, 128)
        cols = pl.ds(base, 128)
        for h in range(2):
            rows = pl.ds(pl.multiple_of(base + h * HEAD_DIM, HEAD_DIM), HEAD_DIM)
            mask = half_mask(h)
            k2, v2 = k_ref[:, cols], v_ref[:, cols]
            km[h] = jnp.where(mask, k2, jnp.zeros_like(k2))
            vm[h] = jnp.where(mask, v2, jnp.zeros_like(v2))
            lane = lax.broadcasted_iota(jnp.int32, (1, 128), 1)
            aux = aux_ref[...]
            head = pair * 2 + h
            lse = jnp.sum(jnp.where(lane == head, aux, 0.0), axis=1, keepdims=True)
            off = jnp.sum(jnp.where(lane == head + HEADS, aux, 0.0), axis=1, keepdims=True)
            lseb[...] = jnp.broadcast_to(lse, (bins, 128))
            offb[...] = jnp.broadcast_to(off, (bins, 128))
            for j in range(blocks):
                ks = slice(j * TILE, (j + 1) * TILE)
                kw, vw = km[h, ks, :], vm[h, ks, :]
                for i in range(j, blocks) if near else range(j + 1):
                    qs = slice(i * TILE, (i + 1) * TILE)
                    p = jnp.exp2(mm(q_ref[qs, cols], kw, 1, 1) - twice(lseb[qs, :]))
                    if i == j:
                        r = lax.broadcasted_iota(jnp.int32, (TILE, TILE), 0)
                        c = lax.broadcasted_iota(jnp.int32, (TILE, TILE), 1)
                        p = jnp.where(r >= c if near else r < c, p, 0.0)
                    dp = mm(do_ref[qs, cols], vw, 1, 1)
                    prob[h, qs, ks] = p.astype(BF16)
                    grad[h, qs, ks] = (p * (dp - twice(offb[qs, :]))).astype(BF16)
            for j in range(blocks):
                ks = slice(j * TILE, (j + 1) * TILE)
                qs = slice(j * TILE, bins) if near else slice(0, (j + 1) * TILE)
                put_value(rows, ks, mm(dot_ref[rows, qs], prob[h, qs, ks], 1, 0))
                put_key(rows, ks, mm(qt_ref[rows, qs], grad[h, qs, ks], 1, 0) * LN2)
            for i in range(blocks):
                qs = slice(i * TILE, (i + 1) * TILE)
                ks = slice(0, (i + 1) * TILE) if near else slice(i * TILE, bins)
                part = mm(grad[h, qs, ks], km[h, ks, :], 1, 0)
                if h == 0:
                    acc[qs, :] = part
                else:
                    put_query(qs, cols, (acc[qs, :] + part) * SCALE)
        return carry

    lax.fori_loop(0, HEADS // 2, body, 0)


def attention_scratch(bins):
    return [
        pltpu.VMEM((2, bins, 128), BF16),
        pltpu.VMEM((2, bins, 128), BF16),
        pltpu.VMEM((bins, 128), F32),
        pltpu.VMEM((bins, 128), F32),
        pltpu.VMEM((2, bins, bins), BF16),
        pltpu.VMEM((2, bins, bins), BF16),
        pltpu.VMEM((bins, 128), F32),
    ]


def near_kernel(
    x_ref, wq_ref, wk_ref, wv_ref, wo_ref, saved_ref, up_ref, lse_ref,
    q_ref, do_ref, qt_ref, dot_ref, aux_ref, dq_ref, dkt_ref, dvt_ref, gwo_ref,
    k_ref, v_ref, *scratch,
):
    bins, width = x_ref.shape
    for b in range(bins // TILE):
        bs = slice(b * TILE, (b + 1) * TILE)
        x = x_ref[bs, :]
        q = (mm(x, wq_ref[...], 1, 0) * (SCALE * LOG2E)).astype(BF16)
        q_ref[bs, :] = q
        qt_ref[:, bs] = q.T
        k_ref[bs, :] = mm(x, wk_ref[...], 1, 0).astype(BF16)
        v_ref[bs, :] = mm(x, wv_ref[...], 1, 0).astype(BF16)
        do = mm(up_ref[bs, :], wo_ref[...], 1, 1).astype(BF16)
        do_ref[bs, :] = do
        dot_ref[:, bs] = do.T
        prod = do.astype(F32) * saved_ref[bs, :].astype(F32)
        lane = lax.broadcasted_iota(jnp.int32, (1, 128), 1)
        padded = jnp.concatenate([lse_ref[:, bs] * LOG2E, jnp.zeros((128 - HEADS, TILE), F32)], axis=0)
        aux = padded.T
        for head in range(HEADS):
            slab = prod[:, head // 2 * 128 : head // 2 * 128 + 128]
            off = jnp.sum(jnp.where(half_mask(head % 2), slab, 0.0), axis=1, keepdims=True)
            aux = jnp.where(lane == HEADS + head, off, aux)
        aux_ref[bs, :] = aux
    gwo_ref[...] = mm(saved_ref[...], up_ref[...], 0, 0).astype(BF16)

    def put_query(qs, cols, value):
        dq_ref[qs, cols] = value

    def put_key(rows, ks, value):
        dkt_ref[rows, ks] = value.astype(BF16)

    def put_value(rows, ks, value):
        dvt_ref[rows, ks] = value.astype(BF16)

    attention(
        True, (q_ref, do_ref, qt_ref, dot_ref, k_ref, v_ref, aux_ref), scratch, put_query, put_key, put_value
    )


def far_kernel(
    x_ref, xp_ref, wk_ref, wv_ref, q_ref, do_ref, qt_ref, dot_ref, aux_ref, dqn_ref, dkt_ref, dvt_ref,
    dq_ref, back_ref, gw_ref,
    k_ref, v_ref, dkf, dvf, xt, xpt, *scratch,
):
    bins, width = x_ref.shape
    for b in range(bins // TILE):
        bs = slice(b * TILE, (b + 1) * TILE)
        xp = xp_ref[bs, :]
        k_ref[bs, :] = mm(xp, wk_ref[...], 1, 0).astype(BF16)
        v_ref[bs, :] = mm(xp, wv_ref[...], 1, 0).astype(BF16)
        xpt[:, bs] = xp.T
        xt[:, bs] = x_ref[bs, :].T

    def put_query(qs, cols, value):
        dq_ref[qs, cols] = (dqn_ref[qs, cols] + value).astype(BF16)

    def put_key(rows, ks, value):
        dkf[rows, ks] = value.astype(BF16)

    def put_value(rows, ks, value):
        dvf[rows, ks] = value.astype(BF16)

    attention(
        False, (q_ref, do_ref, qt_ref, dot_ref, k_ref, v_ref, aux_ref), scratch, put_query, put_key, put_value
    )
    back_ref[...] = (mm(wk_ref[...], dkf[...], 1, 0) + mm(wv_ref[...], dvf[...], 1, 0)).astype(BF16)
    gw_ref[0:width, :] = mm(xt[...], dq_ref[...], 1, 0).astype(BF16)
    gw_ref[width : 2 * width, :] = (mm(xt[...], dkt_ref[...], 1, 1) + mm(xpt[...], dkf[...], 1, 1)).astype(BF16)
    gw_ref[2 * width :, :] = (mm(xt[...], dvt_ref[...], 1, 1) + mm(xpt[...], dvf[...], 1, 1)).astype(BF16)


def input_kernel(dq_ref, dkt_ref, dvt_ref, wq_ref, wk_ref, wv_ref, out_ref):
    out_ref[...] = (
        mm(wq_ref[...], dq_ref[...], 1, 1) + mm(wk_ref[...], dkt_ref[...], 1, 0) + mm(wv_ref[...], dvt_ref[...], 1, 0)
    )


def call(kernel, outs, scratch, flops, *args):
    return pl.pallas_call(
        kernel,
        out_shape=[jax.ShapeDtypeStruct(*o) for o in outs],
        in_specs=[VMEM] * len(args),
        out_specs=[VMEM] * len(outs),
        scratch_shapes=scratch,
        compiler_params=pltpu.CompilerParams(vmem_limit_bytes=48 * 2**20),
        cost_estimate=pl.CostEstimate(
            flops=int(flops), bytes_accessed=sum(a.size * a.dtype.itemsize for a in args), transcendentals=0
        ),
    )(*args)


def scatter_sum(parts, axes):
    me = lax.axis_index(axes)
    count = lax.axis_size(axes)
    keep = parts.astype(F32)
    step = 1
    while step < count:
        halves = keep.reshape(keep.shape[0] // 2, 2, *keep.shape[1:])
        bit = (me // step) % 2
        send = lax.dynamic_index_in_dim(halves, 1 - bit, 1, keepdims=False).astype(BF16)
        keep = lax.dynamic_index_in_dim(halves, bit, 1, keepdims=False)
        got = lax.ppermute(send, axes, [(d, d ^ step) for d in range(count)])
        keep = keep + got.astype(F32)
        step *= 2
    return keep[0]


def on_device(inputs, w_query, w_key, w_value, w_out, saved_heads, log_totals, out_grad):
    x, saved, lse, up = inputs[0], saved_heads[0], log_totals[0], out_grad[0]
    bins, width = x.shape
    tm = lax.axis_size("tm")
    x_prev = lax.ppermute(x, "tm", [(s, s + 1) for s in range(tm - 1)])
    tall, wide, square = (bins, width), (width, bins), (width, width)
    pair = 2 * HEADS * bins * bins * HEAD_DIM * 5
    q, do, qt, dot, aux, dqn, dkt, dvt, gwo = call(
        near_kernel,
        [(tall, BF16), (tall, BF16), (wide, BF16), (wide, BF16), ((bins, 128), F32), (tall, F32), (wide, BF16), (wide, BF16), (square, BF16)],
        [pltpu.VMEM(tall, BF16), pltpu.VMEM(tall, BF16)] + attention_scratch(bins),
        pair,
        x, w_query, w_key, w_value, w_out, saved, up, lse,
    )
    dq, back, gw = call(
        far_kernel,
        [(tall, BF16), (wide, BF16), ((3 * width, width), BF16)],
        [pltpu.VMEM(tall, BF16), pltpu.VMEM(tall, BF16)]
        + [pltpu.VMEM(wide, BF16)] * 4
        + attention_scratch(bins),
        pair,
        x, x_prev, w_key, w_value, q, do, qt, dot, aux, dqn, dkt, dvt,
    )
    back = lax.ppermute(back, "tm", [(s + 1, s) for s in range(tm - 1)])
    (near_grad,) = call(input_kernel, [(wide, F32)], [], 3 * 2 * bins * width * width, dq, dkt, dvt, w_query, w_key, w_value)
    axes = ("dp", "tm")
    count = lax.axis_size(axes)
    parts = jnp.concatenate([gw, gwo], axis=0).reshape(count, 4 * width // count, width)
    weight_grads = scatter_sum(parts, axes)
    input_grad = (near_grad + back.astype(F32)).T.astype(BF16)
    return input_grad[None], weight_grads


def solution(mesh):
    rows, copied = P("dp", "tm", None), P()
    return jax.shard_map(
        on_device,
        mesh=mesh,
        in_specs=(rows, copied, copied, copied, copied, rows, P("dp", None, "tm"), rows),
        out_specs=(rows, P(("dp", "tm"), None)),
        check_vma=False,
    )
```

```python
import functools
import math

import jax
import jax.numpy as jnp
from jax import lax
from jax.experimental import pallas as pl
from jax.experimental.pallas import tpu as pltpu
from jax.sharding import PartitionSpec as P

HEADS = 8
HEAD_DIM = 64
TILE = 256
SCALE = HEAD_DIM**-0.5
LOG2E = math.log2(math.e)
LN2 = math.log(2.0)
F32 = jnp.float32
BF16 = jnp.bfloat16
VMEM = pl.BlockSpec(memory_space=pltpu.VMEM)


def mm(a, b, ca, cb):
    return lax.dot_general(a, b, (((ca,), (cb,)), ((), ())), preferred_element_type=F32)


def twice(x):
    return jnp.concatenate([x, x], axis=1)


def half_mask(h):
    lane = lax.broadcasted_iota(jnp.int32, (1, 128), 1)
    return lane < HEAD_DIM if h == 0 else lane >= HEAD_DIM


def attention(near, refs, scratch, put_query, put_key, put_value):
    q_ref, do_ref, qt_ref, dot_ref, k_ref, v_ref, aux_ref = refs
    km, vm, lseb, offb, prob, grad, acc = scratch
    bins = q_ref.shape[0]
    blocks = bins // TILE

    def body(pair, carry):
        base = pl.multiple_of(pair * 128, 128)
        cols = pl.ds(base, 128)
        for h in range(2):
            rows = pl.ds(pl.multiple_of(base + h * HEAD_DIM, HEAD_DIM), HEAD_DIM)
            mask = half_mask(h)
            k2, v2 = k_ref[:, cols], v_ref[:, cols]
            km[h] = jnp.where(mask, k2, jnp.zeros_like(k2))
            vm[h] = jnp.where(mask, v2, jnp.zeros_like(v2))
            lane = lax.broadcasted_iota(jnp.int32, (1, 128), 1)
            aux = aux_ref[...]
            head = pair * 2 + h
            lse = jnp.sum(jnp.where(lane == head, aux, 0.0), axis=1, keepdims=True)
            off = jnp.sum(jnp.where(lane == head + HEADS, aux, 0.0), axis=1, keepdims=True)
            lseb[...] = jnp.broadcast_to(lse, (bins, 128))
            offb[...] = jnp.broadcast_to(off, (bins, 128))
            for j in range(blocks):
                ks = slice(j * TILE, (j + 1) * TILE)
                kw, vw = km[h, ks, :], vm[h, ks, :]
                for i in range(j, blocks) if near else range(j + 1):
                    qs = slice(i * TILE, (i + 1) * TILE)
                    p = jnp.exp2(mm(q_ref[qs, cols], kw, 1, 1) - twice(lseb[qs, :]))
                    if i == j:
                        r = lax.broadcasted_iota(jnp.int32, (TILE, TILE), 0)
                        c = lax.broadcasted_iota(jnp.int32, (TILE, TILE), 1)
                        p = jnp.where(r >= c if near else r < c, p, 0.0)
                    dp = mm(do_ref[qs, cols], vw, 1, 1)
                    prob[h, qs, ks] = p.astype(BF16)
                    grad[h, qs, ks] = (p * (dp - twice(offb[qs, :]))).astype(BF16)
            for j in range(blocks):
                ks = slice(j * TILE, (j + 1) * TILE)
                qs = slice(j * TILE, bins) if near else slice(0, (j + 1) * TILE)
                put_value(rows, ks, mm(dot_ref[rows, qs], prob[h, qs, ks], 1, 0))
                put_key(rows, ks, mm(qt_ref[rows, qs], grad[h, qs, ks], 1, 0) * LN2)
            for i in range(blocks):
                qs = slice(i * TILE, (i + 1) * TILE)
                ks = slice(0, (i + 1) * TILE) if near else slice(i * TILE, bins)
                part = mm(grad[h, qs, ks], km[h, ks, :], 1, 0)
                if h == 0:
                    acc[qs, :] = part
                else:
                    put_query(qs, cols, (acc[qs, :] + part) * SCALE)
        return carry

    lax.fori_loop(0, HEADS // 2, body, 0)


def attention_scratch(bins):
    return [
        pltpu.VMEM((2, bins, 128), BF16),
        pltpu.VMEM((2, bins, 128), BF16),
        pltpu.VMEM((bins, 128), F32),
        pltpu.VMEM((bins, 128), F32),
        pltpu.VMEM((2, bins, bins), BF16),
        pltpu.VMEM((2, bins, bins), BF16),
        pltpu.VMEM((bins, 128), F32),
    ]


def near_kernel(
    x_hbm, wq_hbm, wk_hbm, wv_hbm, wo_hbm, saved_hbm, up_hbm, lse_hbm,
    q_ref, do_ref, qt_ref, dot_ref, aux_ref, dq_ref, dkt_ref, dvt_ref, gwo_ref, xt_ref, wq_ref, wk_ref, wv_ref,
    x_ref, wo_ref, saved_ref, up_ref, lse_ref, k_ref, v_ref, sems, *scratch,
):
    sources = (up_hbm, wo_hbm, x_hbm, wq_hbm, wk_hbm, wv_hbm, saved_hbm, lse_hbm)
    targets = (up_ref, wo_ref, x_ref, wq_ref, wk_ref, wv_ref, saved_ref, lse_ref)
    copies = [pltpu.make_async_copy(a, b, sems.at[i]) for i, (a, b) in enumerate(zip(sources, targets))]
    for copy in copies:
        copy.start()
    bins, width = x_ref.shape
    tiles = [slice(b * TILE, (b + 1) * TILE) for b in range(bins // TILE)]
    copies[0].wait()
    copies[1].wait()
    for bs in tiles:
        do = mm(up_ref[bs, :], wo_ref[...], 1, 1).astype(BF16)
        do_ref[bs, :] = do
        dot_ref[:, bs] = do.T
    copies[2].wait()
    copies[3].wait()
    for bs in tiles:
        q = (mm(x_ref[bs, :], wq_ref[...], 1, 0) * (SCALE * LOG2E)).astype(BF16)
        q_ref[bs, :] = q
        qt_ref[:, bs] = q.T
        xt_ref[:, bs] = x_ref[bs, :].T
    copies[4].wait()
    copies[5].wait()
    for bs in tiles:
        k_ref[bs, :] = mm(x_ref[bs, :], wk_ref[...], 1, 0).astype(BF16)
        v_ref[bs, :] = mm(x_ref[bs, :], wv_ref[...], 1, 0).astype(BF16)
    copies[6].wait()
    copies[7].wait()
    lane = lax.broadcasted_iota(jnp.int32, (1, 128), 1)
    for bs in tiles:
        prod = do_ref[bs, :].astype(F32) * saved_ref[bs, :].astype(F32)
        padded = jnp.concatenate([lse_ref[:, bs] * LOG2E, jnp.zeros((128 - HEADS, TILE), F32)], axis=0)
        aux = padded.T
        for head in range(HEADS):
            slab = prod[:, head // 2 * 128 : head // 2 * 128 + 128]
            off = jnp.sum(jnp.where(half_mask(head % 2), slab, 0.0), axis=1, keepdims=True)
            aux = jnp.where(lane == HEADS + head, off, aux)
        aux_ref[bs, :] = aux
    gwo_ref[...] = mm(saved_ref[...], up_ref[...], 0, 0)

    def put_query(qs, cols, value):
        dq_ref[qs, cols] = value

    def put_key(rows, ks, value):
        dkt_ref[rows, ks] = value.astype(BF16)

    def put_value(rows, ks, value):
        dvt_ref[rows, ks] = value.astype(BF16)

    attention(
        True, (q_ref, do_ref, qt_ref, dot_ref, k_ref, v_ref, aux_ref), scratch, put_query, put_key, put_value
    )


def far_kernel(
    xp_ref, wk_ref, wv_ref, q_ref, do_ref, qt_ref, dot_ref, aux_ref, dqn_ref,
    dq_ref, back_ref, dkf, dvf, xpt,
    k_ref, v_ref, *scratch,
):
    bins, width = xp_ref.shape
    for b in range(bins // TILE):
        bs = slice(b * TILE, (b + 1) * TILE)
        xp = xp_ref[bs, :]
        k_ref[bs, :] = mm(xp, wk_ref[...], 1, 0).astype(BF16)
        v_ref[bs, :] = mm(xp, wv_ref[...], 1, 0).astype(BF16)
        xpt[:, bs] = xp.T

    def put_query(qs, cols, value):
        dq_ref[qs, cols] = (dqn_ref[qs, cols] + value).astype(BF16)

    def put_key(rows, ks, value):
        dkf[rows, ks] = value.astype(BF16)

    def put_value(rows, ks, value):
        dvf[rows, ks] = value.astype(BF16)

    attention(
        False, (q_ref, do_ref, qt_ref, dot_ref, k_ref, v_ref, aux_ref), scratch, put_query, put_key, put_value
    )
    back_ref[...] = (mm(wk_ref[...], dkf[...], 1, 0) + mm(wv_ref[...], dvf[...], 1, 0)).astype(BF16)


def bit_order(bits, parity):
    rest = list(range(1, bits))
    if parity and len(rest) > 1:
        rest[0], rest[1] = rest[1], rest[0]
    return rest


def place(device, order):
    return sum(((device >> bit) & 1) << (len(order) - 1 - t) for t, bit in enumerate(order))


def weight_kernel(count, xt_ref, xpt_ref, dq_ref, dkt_ref, dvt_ref, dkf_ref, dvf_ref, gwo_ref, send_ref, keep_ref, sums):
    width = xt_ref.shape[0]
    sums[0:width, :] = mm(xt_ref[...], dq_ref[...], 1, 0)
    sums[width : 2 * width, :] = mm(xt_ref[...], dkt_ref[...], 1, 1) + mm(xpt_ref[...], dkf_ref[...], 1, 1)
    sums[2 * width : 3 * width, :] = mm(xt_ref[...], dvt_ref[...], 1, 1) + mm(xpt_ref[...], dvf_ref[...], 1, 1)
    sums[3 * width :, :] = gwo_ref[...]
    rows = 4 * width // count
    bits = count.bit_length() - 1
    mine = lax.axis_index("tm") % 2
    for parity in range(2):

        @pl.when(mine == parity)
        def _(parity=parity):
            for device in range(count):
                at = place(device, bit_order(bits, device & 1))
                block = sums[device * rows : (device + 1) * rows, :]
                if device & 1 == parity:
                    keep_ref[at * rows : (at + 1) * rows, :] = block
                else:
                    send_ref[at * rows : (at + 1) * rows, :] = block.astype(BF16)


def halve_kernel(bit_ref, keep_ref, got_ref, send_ref, out_ref):
    half = out_ref.shape[0]
    bit = bit_ref[0]
    mine = pl.ds(pl.multiple_of(bit * half, half), half)
    other = pl.ds(pl.multiple_of((1 - bit) * half, half), half)
    send_ref[...] = (keep_ref[other, :] + got_ref[other, :].astype(F32)).astype(BF16)
    out_ref[...] = keep_ref[mine, :] + got_ref[mine, :].astype(F32)


def add_kernel(keep_ref, got_ref, out_ref):
    out_ref[...] = keep_ref[...] + got_ref[...].astype(F32)


def near_input_kernel(dq_ref, dkt_ref, dvt_ref, wq_ref, wk_ref, wv_ref, out_ref):
    out_ref[...] = (
        mm(wq_ref[...], dq_ref[...], 1, 1) + mm(wk_ref[...], dkt_ref[...], 1, 0) + mm(wv_ref[...], dvt_ref[...], 1, 0)
    )


def input_kernel(near_ref, back_ref, out_ref):
    bins = out_ref.shape[0]
    for b in range(bins // TILE):
        bs = slice(b * TILE, (b + 1) * TILE)
        out_ref[bs, :] = (near_ref[:, bs] + back_ref[:, bs].astype(F32)).T.astype(BF16)


def call(kernel, outs, scratch, flops, *args, specs=None, limit=24):
    return pl.pallas_call(
        kernel,
        out_shape=outs,
        in_specs=specs or [VMEM] * len(args),
        out_specs=[VMEM] * len(outs),
        scratch_shapes=scratch,
        compiler_params=pltpu.CompilerParams(vmem_limit_bytes=limit * 2**20),
        cost_estimate=pl.CostEstimate(
            flops=int(flops), bytes_accessed=sum(a.size * a.dtype.itemsize for a in args), transcendentals=0
        ),
    )(*args)


def on_chip(x):
    return pltpu.with_memory_space_constraint(x, pltpu.VMEM)


def scatter_sum(send, keep, axes):
    count = lax.axis_size(axes)
    bits = count.bit_length() - 1
    me = lax.axis_index(axes)
    odd = me % 2 == 1
    width = keep.shape[1]
    got = lax.ppermute(send, axes, [(d, d ^ 1) for d in range(count)])
    for even_bit, odd_bit in zip(bit_order(bits, 0), bit_order(bits, 1)):
        half = keep.shape[0] // 2
        bit = jnp.where(odd, me >> odd_bit, me >> even_bit) & 1
        send, keep = call(
            halve_kernel,
            [pltpu.VMEM((half, width), BF16), pltpu.VMEM((half, width), F32)],
            [],
            keep.size,
            bit.reshape(1).astype(jnp.int32),
            on_chip(keep),
            on_chip(got),
            specs=[pl.BlockSpec(memory_space=pltpu.SMEM), VMEM, VMEM],
        )
        steps = (1 << even_bit, 1 << odd_bit)
        got = lax.ppermute(send, axes, [(d, d ^ steps[d & 1]) for d in range(count)])
    (out,) = call(add_kernel, [jax.ShapeDtypeStruct(keep.shape, F32)], [], keep.size, on_chip(keep), on_chip(got))
    return out


def on_device(inputs, w_query, w_key, w_value, w_out, saved_heads, log_totals, out_grad):
    x, saved, lse, up = inputs[0], saved_heads[0], log_totals[0], out_grad[0]
    bins, width = x.shape
    tm = lax.axis_size("tm")
    axes = ("dp", "tm")
    count = lax.axis_size(axes)
    x_prev = lax.ppermute(x, "tm", [(s, s + 1) for s in range(tm - 1)])
    tall, wide, square = (bins, width), (width, bins), (width, width)
    one = 2 * bins * width * width
    band = 2 * HEADS * bins * bins * HEAD_DIM * 5
    q, do, qt, dot, aux, dqn, dkt, dvt, gwo, xt, wq, wk, wv = call(
        near_kernel,
        [pltpu.VMEM(s, d) for s, d in (
            (tall, BF16), (tall, BF16), (wide, BF16), (wide, BF16), ((bins, 128), F32), (tall, F32), (wide, BF16),
            (wide, BF16), (square, F32), (wide, BF16), (square, BF16), (square, BF16), (square, BF16),
        )],
        [pltpu.VMEM(s, d) for s, d in (
            (tall, BF16), (square, BF16), (tall, BF16), (tall, BF16), ((HEADS, bins), F32), (tall, BF16), (tall, BF16),
        )] + [pltpu.SemaphoreType.DMA((8,))] + attention_scratch(bins),
        band,
        x, w_query, w_key, w_value, w_out, saved, up, lse,
        specs=[pl.BlockSpec(memory_space=pltpu.HBM)] * 8,
    )
    dq, back, dkf, dvf, xpt = call(
        far_kernel,
        [pltpu.VMEM(s, BF16) for s in (tall, wide, wide, wide, wide)],
        [pltpu.VMEM(tall, BF16), pltpu.VMEM(tall, BF16)] + attention_scratch(bins),
        band,
        on_chip(x_prev), wk, wv, q, do, qt, dot, aux, dqn,
    )
    back = lax.ppermute(back, "tm", [(s + 1, s) for s in range(tm - 1)])
    half = (2 * width, width)
    send, keep = call(
        functools.partial(weight_kernel, count),
        [pltpu.VMEM(half, BF16), pltpu.VMEM(half, F32)],
        [pltpu.VMEM((4 * width, width), F32)],
        5 * one,
        xt, xpt, dq, dkt, dvt, dkf, dvf, gwo,
    )
    weight_grads = scatter_sum(send, keep, axes)
    (near_grad,) = call(near_input_kernel, [pltpu.VMEM(wide, F32)], [], 3 * one, dq, dkt, dvt, wq, wk, wv)
    (input_grad,) = call(input_kernel, [jax.ShapeDtypeStruct(tall, BF16)], [], one // 8, near_grad, on_chip(back))
    return input_grad[None], weight_grads


def solution(mesh):
    rows, copied = P("dp", "tm", None), P()
    return jax.shard_map(
        on_device,
        mesh=mesh,
        in_specs=(rows, copied, copied, copied, copied, rows, P("dp", None, "tm"), rows),
        out_specs=(rows, P(("dp", "tm"), None)),
        check_vma=False,
    )
```

```python
import functools
import math

import jax
import jax.numpy as jnp
from jax import lax
from jax.experimental import pallas as pl
from jax.experimental.pallas import tpu as pltpu
from jax.sharding import PartitionSpec as P


HEADS = 8
HEAD_DIM = 64
TILE = 256
SCALE = HEAD_DIM**-0.5
LOG2E = math.log2(math.e)
LN2 = math.log(2.0)
F32 = jnp.float32
BF16 = jnp.bfloat16
VMEM = pl.BlockSpec(memory_space=pltpu.VMEM)


def mm(a, b, ca, cb):
    return lax.dot_general(a, b, (((ca,), (cb,)), ((), ())), preferred_element_type=F32)


def twice(x):
    return jnp.concatenate([x, x], axis=1)


def half_mask(h):
    lane = lax.broadcasted_iota(jnp.int32, (1, 128), 1)
    return lane < HEAD_DIM if h == 0 else lane >= HEAD_DIM


def attention(near, refs, scratch, put_query, put_key, put_value):
    q_ref, do_ref, qt_ref, dot_ref, k_ref, v_ref, aux_ref = refs
    km, vm, lseb, offb, prob, grad, acc = scratch
    bins = q_ref.shape[0]
    blocks = bins // TILE

    def body(pair, carry):
        base = pl.multiple_of(pair * 128, 128)
        cols = pl.ds(base, 128)
        for h in range(2):
            rows = pl.ds(pl.multiple_of(base + h * HEAD_DIM, HEAD_DIM), HEAD_DIM)
            mask = half_mask(h)
            k2, v2 = k_ref[:, cols], v_ref[:, cols]
            km[h] = jnp.where(mask, k2, jnp.zeros_like(k2))
            vm[h] = jnp.where(mask, v2, jnp.zeros_like(v2))
            lane = lax.broadcasted_iota(jnp.int32, (1, 128), 1)
            aux = aux_ref[...]
            head = pair * 2 + h
            lse = jnp.sum(jnp.where(lane == head, aux, 0.0), axis=1, keepdims=True)
            off = jnp.sum(jnp.where(lane == head + HEADS, aux, 0.0), axis=1, keepdims=True)
            lseb[...] = jnp.broadcast_to(lse, (bins, 128))
            offb[...] = jnp.broadcast_to(off, (bins, 128))
            for j in range(blocks):
                ks = slice(j * TILE, (j + 1) * TILE)
                kw, vw = km[h, ks, :], vm[h, ks, :]
                for i in range(j, blocks) if near else range(j + 1):
                    qs = slice(i * TILE, (i + 1) * TILE)
                    p = jnp.exp2(mm(q_ref[qs, cols], kw, 1, 1) - twice(lseb[qs, :]))
                    if i == j:
                        r = lax.broadcasted_iota(jnp.int32, (TILE, TILE), 0)
                        c = lax.broadcasted_iota(jnp.int32, (TILE, TILE), 1)
                        p = jnp.where(r >= c if near else r < c, p, 0.0)
                    dp = mm(do_ref[qs, cols], vw, 1, 1)
                    prob[h, qs, ks] = p.astype(BF16)
                    grad[h, qs, ks] = (p * (dp - twice(offb[qs, :]))).astype(BF16)
            for j in range(blocks):
                ks = slice(j * TILE, (j + 1) * TILE)
                qs = slice(j * TILE, bins) if near else slice(0, (j + 1) * TILE)
                put_value(rows, ks, mm(dot_ref[rows, qs], prob[h, qs, ks], 1, 0))
                put_key(rows, ks, mm(qt_ref[rows, qs], grad[h, qs, ks], 1, 0) * LN2)
            for i in range(blocks):
                qs = slice(i * TILE, (i + 1) * TILE)
                ks = slice(0, (i + 1) * TILE) if near else slice(i * TILE, bins)
                part = mm(grad[h, qs, ks], km[h, ks, :], 1, 0)
                if h == 0:
                    acc[qs, :] = part
                else:
                    put_query(qs, cols, (acc[qs, :] + part) * SCALE)
        return carry

    lax.fori_loop(0, HEADS // 2, body, 0)


def attention_scratch(bins):
    return [
        pltpu.VMEM((2, bins, 128), BF16),
        pltpu.VMEM((2, bins, 128), BF16),
        pltpu.VMEM((bins, 128), F32),
        pltpu.VMEM((bins, 128), F32),
        pltpu.VMEM((2, bins, bins), BF16),
        pltpu.VMEM((2, bins, bins), BF16),
        pltpu.VMEM((bins, 128), F32),
    ]


def near_kernel(
    x_hbm, wq_hbm, wk_hbm, wv_hbm, wo_hbm, saved_hbm, up_hbm, lse_hbm,
    q_ref, do_ref, qt_ref, dot_ref, aux_ref, dq_ref, dkt_ref, dvt_ref, gwo_ref, xt_ref, wq_ref, wk_ref, wv_ref,
    x_ref, wo_ref, saved_ref, up_ref, lse_ref, k_ref, v_ref, sems, *scratch,
):
    sources = (up_hbm, wo_hbm, x_hbm, wq_hbm, wk_hbm, wv_hbm, saved_hbm, lse_hbm)
    targets = (up_ref, wo_ref, x_ref, wq_ref, wk_ref, wv_ref, saved_ref, lse_ref)
    copies = [pltpu.make_async_copy(a, b, sems.at[i]) for i, (a, b) in enumerate(zip(sources, targets))]
    for copy in copies:
        copy.start()
    bins, _ = x_ref.shape
    tiles = [slice(b * TILE, (b + 1) * TILE) for b in range(bins // TILE)]
    copies[0].wait()
    copies[1].wait()
    for bs in tiles:
        do = mm(up_ref[bs, :], wo_ref[...], 1, 1).astype(BF16)
        do_ref[bs, :] = do
        dot_ref[:, bs] = do.T
    copies[2].wait()
    copies[3].wait()
    for bs in tiles:
        q = (mm(x_ref[bs, :], wq_ref[...], 1, 0) * (SCALE * LOG2E)).astype(BF16)
        q_ref[bs, :] = q
        qt_ref[:, bs] = q.T
        xt_ref[:, bs] = x_ref[bs, :].T
    copies[4].wait()
    copies[5].wait()
    for bs in tiles:
        k_ref[bs, :] = mm(x_ref[bs, :], wk_ref[...], 1, 0).astype(BF16)
        v_ref[bs, :] = mm(x_ref[bs, :], wv_ref[...], 1, 0).astype(BF16)
    copies[6].wait()
    copies[7].wait()
    lane = lax.broadcasted_iota(jnp.int32, (1, 128), 1)
    for bs in tiles:
        prod = do_ref[bs, :].astype(F32) * saved_ref[bs, :].astype(F32)
        padded = jnp.concatenate([lse_ref[:, bs] * LOG2E, jnp.zeros((128 - HEADS, TILE), F32)], axis=0)
        aux = padded.T
        for head in range(HEADS):
            slab = prod[:, head // 2 * 128 : head // 2 * 128 + 128]
            off = jnp.sum(jnp.where(half_mask(head % 2), slab, 0.0), axis=1, keepdims=True)
            aux = jnp.where(lane == HEADS + head, off, aux)
        aux_ref[bs, :] = aux
    gwo_ref[...] = mm(saved_ref[...], up_ref[...], 0, 0)

    def put_query(qs, cols, value):
        dq_ref[qs, cols] = value

    def put_key(rows, ks, value):
        dkt_ref[rows, ks] = value.astype(BF16)

    def put_value(rows, ks, value):
        dvt_ref[rows, ks] = value.astype(BF16)

    attention(
        True, (q_ref, do_ref, qt_ref, dot_ref, k_ref, v_ref, aux_ref), scratch, put_query, put_key, put_value
    )


def far_kernel(
    xp_ref, wk_ref, wv_ref, q_ref, do_ref, qt_ref, dot_ref, aux_ref, dqn_ref,
    dq_ref, back_ref, dkf, dvf, xpt,
    k_ref, v_ref, *scratch,
):
    bins, _ = xp_ref.shape
    for b in range(bins // TILE):
        bs = slice(b * TILE, (b + 1) * TILE)
        xp = xp_ref[bs, :]
        k_ref[bs, :] = mm(xp, wk_ref[...], 1, 0).astype(BF16)
        v_ref[bs, :] = mm(xp, wv_ref[...], 1, 0).astype(BF16)
        xpt[:, bs] = xp.T

    def put_query(qs, cols, value):
        dq_ref[qs, cols] = (dqn_ref[qs, cols] + value).astype(BF16)

    def put_key(rows, ks, value):
        dkf[rows, ks] = value.astype(BF16)

    def put_value(rows, ks, value):
        dvf[rows, ks] = value.astype(BF16)

    attention(
        False, (q_ref, do_ref, qt_ref, dot_ref, k_ref, v_ref, aux_ref), scratch, put_query, put_key, put_value
    )
    back_ref[...] = (mm(wk_ref[...], dkf[...], 1, 0) + mm(wv_ref[...], dvf[...], 1, 0)).astype(BF16)


def bit_order(bits, parity):
    rest = list(range(1, bits))
    if parity and len(rest) > 1:
        rest[0], rest[1] = rest[1], rest[0]
    return rest


def place(device, order):
    return sum(((device >> bit) & 1) << (len(order) - 1 - t) for t, bit in enumerate(order))


def weight_kernel(count, xt_ref, xpt_ref, dq_ref, dkt_ref, dvt_ref, dkf_ref, dvf_ref, gwo_ref, send_ref, keep_ref, sums):
    width = xt_ref.shape[0]
    sums[0:width, :] = mm(xt_ref[...], dq_ref[...], 1, 0)
    sums[width : 2 * width, :] = mm(xt_ref[...], dkt_ref[...], 1, 1) + mm(xpt_ref[...], dkf_ref[...], 1, 1)
    sums[2 * width : 3 * width, :] = mm(xt_ref[...], dvt_ref[...], 1, 1) + mm(xpt_ref[...], dvf_ref[...], 1, 1)
    sums[3 * width :, :] = gwo_ref[...]
    rows = 4 * width // count
    bits = count.bit_length() - 1
    mine = lax.axis_index("tm") % 2
    for parity in range(2):

        @pl.when(mine == parity)
        def _(parity=parity):
            for device in range(count):
                at = place(device, bit_order(bits, device & 1))
                block = sums[device * rows : (device + 1) * rows, :]
                if device & 1 == parity:
                    keep_ref[at * rows : (at + 1) * rows, :] = block
                else:
                    send_ref[at * rows : (at + 1) * rows, :] = block.astype(BF16)


def halve_kernel(even_bit, odd_bit, keep_ref, got_ref, send_ref, out_ref):
    half = out_ref.shape[0]
    me = lax.axis_index(("dp", "tm"))
    bit = jnp.where(me % 2 == 1, me >> odd_bit, me >> even_bit) & 1
    mine = pl.ds(pl.multiple_of(bit * half, half), half)
    other = pl.ds(pl.multiple_of((1 - bit) * half, half), half)
    send_ref[...] = (keep_ref[other, :] + got_ref[other, :].astype(F32)).astype(BF16)
    out_ref[...] = keep_ref[mine, :] + got_ref[mine, :].astype(F32)


def add_kernel(keep_ref, got_ref, out_ref):
    out_ref[...] = keep_ref[...] + got_ref[...].astype(F32)


def near_input_kernel(dq_ref, dkt_ref, dvt_ref, wq_ref, wk_ref, wv_ref, out_ref):
    out_ref[...] = (
        mm(wq_ref[...], dq_ref[...], 1, 1) + mm(wk_ref[...], dkt_ref[...], 1, 0) + mm(wv_ref[...], dvt_ref[...], 1, 0)
    )


def input_kernel(near_ref, back_ref, out_ref):
    bins = out_ref.shape[0]
    for b in range(bins // TILE):
        bs = slice(b * TILE, (b + 1) * TILE)
        out_ref[bs, :] = (near_ref[:, bs] + back_ref[:, bs].astype(F32)).T.astype(BF16)


def call(kernel, outs, scratch, flops, *args, specs=None, limit=24):
    return pl.pallas_call(
        kernel,
        out_shape=outs,
        in_specs=specs or [VMEM] * len(args),
        out_specs=[VMEM] * len(outs),
        scratch_shapes=scratch,
        compiler_params=pltpu.CompilerParams(vmem_limit_bytes=limit * 2**20),
        cost_estimate=pl.CostEstimate(
            flops=int(flops), bytes_accessed=sum(a.size * a.dtype.itemsize for a in args), transcendentals=0
        ),
    )(*args)


def on_chip(x):
    return pltpu.with_memory_space_constraint(x, pltpu.VMEM)


def scatter_sum(send, keep, axes):
    count = lax.axis_size(axes)
    bits = count.bit_length() - 1
    width = keep.shape[1]
    got = lax.ppermute(send, axes, [(d, d ^ 1) for d in range(count)])
    for even_bit, odd_bit in zip(bit_order(bits, 0), bit_order(bits, 1)):
        half = keep.shape[0] // 2
        send, keep = call(
            functools.partial(halve_kernel, even_bit, odd_bit),
            [pltpu.VMEM((half, width), BF16), pltpu.VMEM((half, width), F32)],
            [],
            keep.size,
            on_chip(keep),
            on_chip(got),
        )
        steps = (1 << even_bit, 1 << odd_bit)
        got = lax.ppermute(send, axes, [(d, d ^ steps[d & 1]) for d in range(count)])
    (out,) = call(add_kernel, [jax.ShapeDtypeStruct(keep.shape, F32)], [], keep.size, on_chip(keep), on_chip(got))
    return out


def on_device(inputs, w_query, w_key, w_value, w_out, saved_heads, log_totals, out_grad):
    x, saved, lse, up = inputs[0], saved_heads[0], log_totals[0], out_grad[0]
    bins, width = x.shape
    tm = lax.axis_size("tm")
    axes = ("dp", "tm")
    count = lax.axis_size(axes)
    x_prev = lax.ppermute(x, "tm", [(s, s + 1) for s in range(tm - 1)])
    tall, wide, square = (bins, width), (width, bins), (width, width)
    one = 2 * bins * width * width
    band = 2 * HEADS * bins * bins * HEAD_DIM * 5
    q, do, qt, dot, aux, dqn, dkt, dvt, gwo, xt, wq, wk, wv = call(
        near_kernel,
        [pltpu.VMEM(s, d) for s, d in (
            (tall, BF16), (tall, BF16), (wide, BF16), (wide, BF16), ((bins, 128), F32), (tall, F32), (wide, BF16),
            (wide, BF16), (square, F32), (wide, BF16), (square, BF16), (square, BF16), (square, BF16),
        )],
        [pltpu.VMEM(s, d) for s, d in (
            (tall, BF16), (square, BF16), (tall, BF16), (tall, BF16), ((HEADS, bins), F32), (tall, BF16), (tall, BF16),
        )] + [pltpu.SemaphoreType.DMA((8,))] + attention_scratch(bins),
        band,
        *[pltpu.with_memory_space_constraint(a, pltpu.HBM) for a in (x, w_query, w_key, w_value, w_out, saved, up, lse)],
        specs=[pl.BlockSpec(memory_space=pltpu.HBM)] * 8,
    )
    dq, back, dkf, dvf, xpt = call(
        far_kernel,
        [pltpu.VMEM(s, BF16) for s in (tall, wide, wide, wide, wide)],
        [pltpu.VMEM(tall, BF16), pltpu.VMEM(tall, BF16)] + attention_scratch(bins),
        band,
        on_chip(x_prev), wk, wv, q, do, qt, dot, aux, dqn,
    )
    back = lax.ppermute(back, "tm", [(s + 1, s) for s in range(tm - 1)])
    half = (2 * width, width)
    send, keep = call(
        functools.partial(weight_kernel, count),
        [pltpu.VMEM(half, BF16), pltpu.VMEM(half, F32)],
        [pltpu.VMEM((4 * width, width), F32)],
        5 * one,
        xt, xpt, dq, dkt, dvt, dkf, dvf, gwo,
    )
    weight_grads = scatter_sum(send, keep, axes)
    (near_grad,) = call(near_input_kernel, [pltpu.VMEM(wide, F32)], [], 3 * one, dq, dkt, dvt, wq, wk, wv)
    (input_grad,) = call(input_kernel, [jax.ShapeDtypeStruct(tall, BF16)], [], one // 8, near_grad, on_chip(back))
    return input_grad[None], weight_grads


def solution(mesh):
    rows, copied = P("dp", "tm", None), P()

    return jax.shard_map(
        on_device,
        mesh=mesh,
        in_specs=(rows, copied, copied, copied, copied, rows, P("dp", None, "tm"), rows),
        out_specs=(rows, P(("dp", "tm"), None)),
        check_vma=False,
    )
```

```python
import functools
import math

import jax
import jax.numpy as jnp
from jax import lax
from jax.experimental import pallas as pl
from jax.experimental.pallas import tpu as pltpu
from jax.sharding import PartitionSpec as P


HEADS = 8
HEAD_DIM = 64
TILE = 256
SCALE = HEAD_DIM**-0.5
LOG2E = math.log2(math.e)
LN2 = math.log(2.0)
F32 = jnp.float32
BF16 = jnp.bfloat16
VMEM = pl.BlockSpec(memory_space=pltpu.VMEM)


def mm(a, b, ca, cb):
    return lax.dot_general(a, b, (((ca,), (cb,)), ((), ())), preferred_element_type=F32)


def twice(x):
    return jnp.concatenate([x, x], axis=1)


def half_mask(h):
    lane = lax.broadcasted_iota(jnp.int32, (1, 128), 1)
    return lane < HEAD_DIM if h == 0 else lane >= HEAD_DIM


def attention(near, refs, scratch, put_query, put_key, put_value):
    q_ref, do_ref, qt_ref, dot_ref, k_ref, v_ref, aux_ref = refs
    km, vm, lseb, offb, prob, grad, acc = scratch
    bins = q_ref.shape[0]
    blocks = bins // TILE

    def body(pair, carry):
        base = pl.multiple_of(pair * 128, 128)
        cols = pl.ds(base, 128)
        for h in range(2):
            rows = pl.ds(pl.multiple_of(base + h * HEAD_DIM, HEAD_DIM), HEAD_DIM)
            mask = half_mask(h)
            k2, v2 = k_ref[:, cols], v_ref[:, cols]
            km[h] = jnp.where(mask, k2, jnp.zeros_like(k2))
            vm[h] = jnp.where(mask, v2, jnp.zeros_like(v2))
            lane = lax.broadcasted_iota(jnp.int32, (1, 128), 1)
            aux = aux_ref[...]
            head = pair * 2 + h
            lse = jnp.sum(jnp.where(lane == head, aux, 0.0), axis=1, keepdims=True)
            off = jnp.sum(jnp.where(lane == head + HEADS, aux, 0.0), axis=1, keepdims=True)
            lseb[...] = jnp.broadcast_to(lse, (bins, 128))
            offb[...] = jnp.broadcast_to(off, (bins, 128))
            for j in range(blocks):
                ks = slice(j * TILE, (j + 1) * TILE)
                kw, vw = km[h, ks, :], vm[h, ks, :]
                for i in range(j, blocks) if near else range(j + 1):
                    qs = slice(i * TILE, (i + 1) * TILE)
                    p = jnp.exp2(mm(q_ref[qs, cols], kw, 1, 1) - twice(lseb[qs, :]))
                    if i == j:
                        r = lax.broadcasted_iota(jnp.int32, (TILE, TILE), 0)
                        c = lax.broadcasted_iota(jnp.int32, (TILE, TILE), 1)
                        p = jnp.where(r >= c if near else r < c, p, 0.0)
                    dp = mm(do_ref[qs, cols], vw, 1, 1)
                    prob[h, qs, ks] = p.astype(BF16)
                    grad[h, qs, ks] = (p * (dp - twice(offb[qs, :]))).astype(BF16)
            for j in range(blocks):
                ks = slice(j * TILE, (j + 1) * TILE)
                qs = slice(j * TILE, bins) if near else slice(0, (j + 1) * TILE)
                put_value(rows, ks, mm(dot_ref[rows, qs], prob[h, qs, ks], 1, 0))
                put_key(rows, ks, mm(qt_ref[rows, qs], grad[h, qs, ks], 1, 0) * LN2)
            for i in range(blocks):
                qs = slice(i * TILE, (i + 1) * TILE)
                ks = slice(0, (i + 1) * TILE) if near else slice(i * TILE, bins)
                part = mm(grad[h, qs, ks], km[h, ks, :], 1, 0)
                if h == 0:
                    acc[qs, :] = part
                else:
                    put_query(qs, cols, (acc[qs, :] + part) * SCALE)
        return carry

    lax.fori_loop(0, HEADS // 2, body, 0)


def attention_scratch(bins):
    return [
        pltpu.VMEM((2, bins, 128), BF16),
        pltpu.VMEM((2, bins, 128), BF16),
        pltpu.VMEM((bins, 128), F32),
        pltpu.VMEM((bins, 128), F32),
        pltpu.VMEM((2, bins, bins), BF16),
        pltpu.VMEM((2, bins, bins), BF16),
        pltpu.VMEM((bins, 128), F32),
    ]


def near_kernel(
    x_hbm, wq_hbm, wk_hbm, wv_hbm, wo_hbm, saved_hbm, up_hbm, lse_hbm,
    q_ref, do_ref, qt_ref, dot_ref, aux_ref, dq_ref, dkt_ref, dvt_ref, gwo_ref, xt_ref, wq_ref, wk_ref, wv_ref,
    x_ref, wo_ref, saved_ref, up_ref, lse_ref, k_ref, v_ref, sems, *scratch,
):
    sources = (up_hbm, wo_hbm, x_hbm, wq_hbm, wk_hbm, wv_hbm, saved_hbm, lse_hbm)
    targets = (up_ref, wo_ref, x_ref, wq_ref, wk_ref, wv_ref, saved_ref, lse_ref)
    copies = [pltpu.make_async_copy(a, b, sems.at[i]) for i, (a, b) in enumerate(zip(sources, targets))]
    for copy in copies:
        copy.start()
    bins, _ = x_ref.shape
    tiles = [slice(b * TILE, (b + 1) * TILE) for b in range(bins // TILE)]
    copies[0].wait()
    copies[1].wait()
    for bs in tiles:
        do = mm(up_ref[bs, :], wo_ref[...], 1, 1).astype(BF16)
        do_ref[bs, :] = do
        dot_ref[:, bs] = do.T
    copies[2].wait()
    copies[3].wait()
    for bs in tiles:
        q = (mm(x_ref[bs, :], wq_ref[...], 1, 0) * (SCALE * LOG2E)).astype(BF16)
        q_ref[bs, :] = q
        qt_ref[:, bs] = q.T
        xt_ref[:, bs] = x_ref[bs, :].T
    copies[4].wait()
    copies[5].wait()
    for bs in tiles:
        k_ref[bs, :] = mm(x_ref[bs, :], wk_ref[...], 1, 0).astype(BF16)
        v_ref[bs, :] = mm(x_ref[bs, :], wv_ref[...], 1, 0).astype(BF16)
    copies[6].wait()
    copies[7].wait()
    lane = lax.broadcasted_iota(jnp.int32, (1, 128), 1)
    for bs in tiles:
        prod = do_ref[bs, :].astype(F32) * saved_ref[bs, :].astype(F32)
        padded = jnp.concatenate([lse_ref[:, bs] * LOG2E, jnp.zeros((128 - HEADS, TILE), F32)], axis=0)
        aux = padded.T
        for head in range(HEADS):
            slab = prod[:, head // 2 * 128 : head // 2 * 128 + 128]
            off = jnp.sum(jnp.where(half_mask(head % 2), slab, 0.0), axis=1, keepdims=True)
            aux = jnp.where(lane == HEADS + head, off, aux)
        aux_ref[bs, :] = aux
    gwo_ref[...] = mm(saved_ref[...], up_ref[...], 0, 0)

    def put_query(qs, cols, value):
        dq_ref[qs, cols] = value

    def put_key(rows, ks, value):
        dkt_ref[rows, ks] = value.astype(BF16)

    def put_value(rows, ks, value):
        dvt_ref[rows, ks] = value.astype(BF16)

    attention(
        True, (q_ref, do_ref, qt_ref, dot_ref, k_ref, v_ref, aux_ref), scratch, put_query, put_key, put_value
    )


def far_kernel(
    xp_ref, wk_ref, wv_ref, q_ref, do_ref, qt_ref, dot_ref, aux_ref, dqn_ref,
    dq_ref, dkf, dvf, xpt,
    k_ref, v_ref, *scratch,
):
    bins, _ = xp_ref.shape
    for b in range(bins // TILE):
        bs = slice(b * TILE, (b + 1) * TILE)
        xp = xp_ref[bs, :]
        k_ref[bs, :] = mm(xp, wk_ref[...], 1, 0).astype(BF16)
        v_ref[bs, :] = mm(xp, wv_ref[...], 1, 0).astype(BF16)
        xpt[:, bs] = xp.T

    def put_query(qs, cols, value):
        dq_ref[qs, cols] = (dqn_ref[qs, cols] + value).astype(BF16)

    def put_key(rows, ks, value):
        dkf[rows, ks] = value.astype(BF16)

    def put_value(rows, ks, value):
        dvf[rows, ks] = value.astype(BF16)

    attention(
        False, (q_ref, do_ref, qt_ref, dot_ref, k_ref, v_ref, aux_ref), scratch, put_query, put_key, put_value
    )


def back_kernel(dkf_ref, dvf_ref, wk_ref, wv_ref, out_ref):
    out_ref[...] = (mm(wk_ref[...], dkf_ref[...], 1, 0) + mm(wv_ref[...], dvf_ref[...], 1, 0)).astype(BF16)


def bit_order(bits, parity):
    rest = list(range(1, bits))
    turn = (2, 1, 0) if parity == 0 else (1, 2, 0)
    return [rest[t] for t in turn] + rest[3:] if len(rest) >= 3 else rest


def place(device, order):
    return sum(((device >> bit) & 1) << (len(order) - 1 - t) for t, bit in enumerate(order))


def weight_kernel(count, xt_ref, xpt_ref, dq_ref, dkt_ref, dvt_ref, dkf_ref, dvf_ref, gwo_ref, send_ref, keep_ref, sums):
    width = xt_ref.shape[0]
    sums[0:width, :] = mm(xt_ref[...], dq_ref[...], 1, 0)
    sums[width : 2 * width, :] = mm(xt_ref[...], dkt_ref[...], 1, 1) + mm(xpt_ref[...], dkf_ref[...], 1, 1)
    sums[2 * width : 3 * width, :] = mm(xt_ref[...], dvt_ref[...], 1, 1) + mm(xpt_ref[...], dvf_ref[...], 1, 1)
    sums[3 * width :, :] = gwo_ref[...]
    rows = 4 * width // count
    bits = count.bit_length() - 1
    mine = lax.axis_index("tm") % 2
    for parity in range(2):

        @pl.when(mine == parity)
        def _(parity=parity):
            for device in range(count):
                at = place(device, bit_order(bits, device & 1))
                block = sums[device * rows : (device + 1) * rows, :]
                if device & 1 == parity:
                    keep_ref[at * rows : (at + 1) * rows, :] = block
                else:
                    send_ref[at * rows : (at + 1) * rows, :] = block.astype(BF16)


def halve_kernel(even_bit, odd_bit, keep_ref, got_ref, send_ref, out_ref):
    half = out_ref.shape[0]
    me = lax.axis_index(("dp", "tm"))
    bit = jnp.where(me % 2 == 1, me >> odd_bit, me >> even_bit) & 1
    mine = pl.ds(pl.multiple_of(bit * half, half), half)
    other = pl.ds(pl.multiple_of((1 - bit) * half, half), half)
    send_ref[...] = (keep_ref[other, :] + got_ref[other, :].astype(F32)).astype(BF16)
    out_ref[...] = keep_ref[mine, :] + got_ref[mine, :].astype(F32)


def add_kernel(keep_ref, got_ref, out_ref):
    out_ref[...] = keep_ref[...] + got_ref[...].astype(F32)


def near_input_kernel(dq_ref, dkt_ref, dvt_ref, wq_ref, wk_ref, wv_ref, out_ref):
    out_ref[...] = (
        mm(wq_ref[...], dq_ref[...], 1, 1) + mm(wk_ref[...], dkt_ref[...], 1, 0) + mm(wv_ref[...], dvt_ref[...], 1, 0)
    )


def input_kernel(near_ref, back_ref, out_ref):
    bins = out_ref.shape[0]
    for b in range(bins // TILE):
        bs = slice(b * TILE, (b + 1) * TILE)
        out_ref[bs, :] = (near_ref[:, bs] + back_ref[:, bs].astype(F32)).T.astype(BF16)


def call(kernel, outs, scratch, flops, *args, specs=None, limit=24):
    return pl.pallas_call(
        kernel,
        out_shape=outs,
        in_specs=specs or [VMEM] * len(args),
        out_specs=[VMEM] * len(outs),
        scratch_shapes=scratch,
        compiler_params=pltpu.CompilerParams(vmem_limit_bytes=limit * 2**20),
        cost_estimate=pl.CostEstimate(
            flops=int(flops), bytes_accessed=sum(a.size * a.dtype.itemsize for a in args), transcendentals=0
        ),
    )(*args)


def on_chip(x):
    return pltpu.with_memory_space_constraint(x, pltpu.VMEM)


def scatter_sum(send, keep, axes):
    count = lax.axis_size(axes)
    bits = count.bit_length() - 1
    width = keep.shape[1]
    got = lax.ppermute(send, axes, [(d, d ^ 1) for d in range(count)])
    for even_bit, odd_bit in zip(bit_order(bits, 0), bit_order(bits, 1)):
        half = keep.shape[0] // 2
        send, keep = call(
            functools.partial(halve_kernel, even_bit, odd_bit),
            [pltpu.VMEM((half, width), BF16), pltpu.VMEM((half, width), F32)],
            [],
            keep.size,
            on_chip(keep),
            on_chip(got),
        )
        steps = (1 << even_bit, 1 << odd_bit)
        got = lax.ppermute(send, axes, [(d, d ^ steps[d & 1]) for d in range(count)])
    (out,) = call(add_kernel, [jax.ShapeDtypeStruct(keep.shape, F32)], [], keep.size, on_chip(keep), on_chip(got))
    return out


def on_device(inputs, w_query, w_key, w_value, w_out, saved_heads, log_totals, out_grad):
    x, saved, lse, up = inputs[0], saved_heads[0], log_totals[0], out_grad[0]
    bins, width = x.shape
    tm = lax.axis_size("tm")
    axes = ("dp", "tm")
    count = lax.axis_size(axes)
    x_prev = lax.ppermute(x, "tm", [(s, s + 1) for s in range(tm - 1)])
    tall, wide, square = (bins, width), (width, bins), (width, width)
    one = 2 * bins * width * width
    band = 2 * HEADS * bins * bins * HEAD_DIM * 5
    q, do, qt, dot, aux, dqn, dkt, dvt, gwo, xt, wq, wk, wv = call(
        near_kernel,
        [pltpu.VMEM(s, d) for s, d in (
            (tall, BF16), (tall, BF16), (wide, BF16), (wide, BF16), ((bins, 128), F32), (tall, F32), (wide, BF16),
            (wide, BF16), (square, F32), (wide, BF16), (square, BF16), (square, BF16), (square, BF16),
        )],
        [pltpu.VMEM(s, d) for s, d in (
            (tall, BF16), (square, BF16), (tall, BF16), (tall, BF16), ((HEADS, bins), F32), (tall, BF16), (tall, BF16),
        )] + [pltpu.SemaphoreType.DMA((8,))] + attention_scratch(bins),
        band,
        *[pltpu.with_memory_space_constraint(a, pltpu.HBM) for a in (x, w_query, w_key, w_value, w_out, saved, up, lse)],
        specs=[pl.BlockSpec(memory_space=pltpu.HBM)] * 8,
    )
    dq, dkf, dvf, xpt = call(
        far_kernel,
        [pltpu.VMEM(s, BF16) for s in (tall, wide, wide, wide)],
        [pltpu.VMEM(tall, BF16), pltpu.VMEM(tall, BF16)] + attention_scratch(bins),
        band,
        on_chip(x_prev), wk, wv, q, do, qt, dot, aux, dqn,
    )
    half = (2 * width, width)
    send, keep = call(
        functools.partial(weight_kernel, count),
        [pltpu.VMEM(half, BF16), pltpu.VMEM(half, F32)],
        [pltpu.VMEM((4 * width, width), F32)],
        5 * one,
        xt, xpt, dq, dkt, dvt, dkf, dvf, gwo,
    )
    (back,) = call(back_kernel, [pltpu.VMEM(wide, BF16)], [], 2 * one, dkf, dvf, wk, wv)
    back = lax.ppermute(back, "tm", [(s + 1, s) for s in range(tm - 1)])
    weight_grads = scatter_sum(send, keep, axes)
    (near_grad,) = call(near_input_kernel, [pltpu.VMEM(wide, F32)], [], 3 * one, dq, dkt, dvt, wq, wk, wv)
    (input_grad,) = call(input_kernel, [jax.ShapeDtypeStruct(tall, BF16)], [], one // 8, near_grad, on_chip(back))
    return input_grad[None], weight_grads


def solution(mesh):
    rows, copied = P("dp", "tm", None), P()

    return jax.shard_map(
        on_device,
        mesh=mesh,
        in_specs=(rows, copied, copied, copied, copied, rows, P("dp", None, "tm"), rows),
        out_specs=(rows, P(("dp", "tm"), None)),
        check_vma=False,
    )
```

```python
import functools
import math

import jax
import jax.numpy as jnp
from jax import lax
from jax.experimental import pallas as pl
from jax.experimental.pallas import tpu as pltpu
from jax.sharding import PartitionSpec as P


HEADS = 8
HEAD_DIM = 64
TILE = 256
SCALE = HEAD_DIM**-0.5
LOG2E = math.log2(math.e)
LN2 = math.log(2.0)
F32 = jnp.float32
BF16 = jnp.bfloat16
VMEM = pl.BlockSpec(memory_space=pltpu.VMEM)


def mm(a, b, ca, cb):
    return lax.dot_general(a, b, (((ca,), (cb,)), ((), ())), preferred_element_type=F32)


def twice(x):
    return jnp.concatenate([x, x], axis=1)


def half_mask(h):
    lane = lax.broadcasted_iota(jnp.int32, (1, 128), 1)
    return lane < HEAD_DIM if h == 0 else lane >= HEAD_DIM


def attention(near, refs, scratch, put_query, put_key, put_value):
    q_ref, do_ref, qt_ref, dot_ref, k_ref, v_ref, kt_ref, aux_ref = refs
    km, vm, lseb, offb, prob, grad, grad_t = scratch
    bins = q_ref.shape[0]
    blocks = bins // TILE

    def body(pair, carry):
        base = pl.multiple_of(pair * 128, 128)
        cols = pl.ds(base, 128)
        for h in range(2):
            rows = pl.ds(pl.multiple_of(base + h * HEAD_DIM, HEAD_DIM), HEAD_DIM)
            mask = half_mask(h)
            k2, v2 = k_ref[:, cols], v_ref[:, cols]
            km[h] = jnp.where(mask, k2, jnp.zeros_like(k2))
            vm[h] = jnp.where(mask, v2, jnp.zeros_like(v2))
            lane = lax.broadcasted_iota(jnp.int32, (1, 128), 1)
            aux = aux_ref[...]
            head = pair * 2 + h
            lse = jnp.sum(jnp.where(lane == head, aux, 0.0), axis=1, keepdims=True)
            off = jnp.sum(jnp.where(lane == head + HEADS, aux, 0.0), axis=1, keepdims=True)
            lseb[...] = jnp.broadcast_to(lse, (bins, 128))
            offb[...] = jnp.broadcast_to(off, (bins, 128))
            for j in range(blocks):
                ks = slice(j * TILE, (j + 1) * TILE)
                kw, vw = km[h, ks, :], vm[h, ks, :]
                for i in range(j, blocks) if near else range(j + 1):
                    qs = slice(i * TILE, (i + 1) * TILE)
                    p = jnp.exp2(mm(q_ref[qs, cols], kw, 1, 1) - twice(lseb[qs, :]))
                    if i == j:
                        r = lax.broadcasted_iota(jnp.int32, (TILE, TILE), 0)
                        c = lax.broadcasted_iota(jnp.int32, (TILE, TILE), 1)
                        p = jnp.where(r >= c if near else r < c, p, 0.0)
                    dp = mm(do_ref[qs, cols], vw, 1, 1)
                    prob[h, qs, ks] = p.astype(BF16)
                    g = (p * (dp - twice(offb[qs, :]))).astype(BF16)
                    grad[h, qs, ks] = g
                    grad_t[h, ks, qs] = g.T
            for j in range(blocks):
                ks = slice(j * TILE, (j + 1) * TILE)
                qs = slice(j * TILE, bins) if near else slice(0, (j + 1) * TILE)
                put_value(rows, ks, mm(dot_ref[rows, qs], prob[h, qs, ks], 1, 0))
                put_key(rows, ks, mm(qt_ref[rows, qs], grad[h, qs, ks], 1, 0) * LN2)
            for i in range(blocks):
                qs = slice(i * TILE, (i + 1) * TILE)
                ks = slice(0, (i + 1) * TILE) if near else slice(i * TILE, bins)
                put_query(rows, qs, mm(kt_ref[rows, ks], grad_t[h, ks, qs], 1, 0) * SCALE)
        return carry

    lax.fori_loop(0, HEADS // 2, body, 0)


def attention_scratch(bins):
    return [
        pltpu.VMEM((2, bins, 128), BF16),
        pltpu.VMEM((2, bins, 128), BF16),
        pltpu.VMEM((bins, 128), F32),
        pltpu.VMEM((bins, 128), F32),
        pltpu.VMEM((2, bins, bins), BF16),
        pltpu.VMEM((2, bins, bins), BF16),
        pltpu.VMEM((2, bins, bins), BF16),
    ]


def near_kernel(
    x_hbm, wq_hbm, wk_hbm, wv_hbm, wo_hbm, saved_hbm, up_hbm, lse_hbm,
    q_ref, do_ref, qt_ref, dot_ref, aux_ref, dqt_ref, dkt_ref, dvt_ref, gwo_ref, xt_ref, wq_ref, wk_ref, wv_ref,
    x_ref, wo_ref, saved_ref, up_ref, lse_ref, k_ref, v_ref, kt_ref, sems, *scratch,
):
    sources = (up_hbm, wo_hbm, x_hbm, wq_hbm, wk_hbm, wv_hbm, saved_hbm, lse_hbm)
    targets = (up_ref, wo_ref, x_ref, wq_ref, wk_ref, wv_ref, saved_ref, lse_ref)
    copies = [pltpu.make_async_copy(a, b, sems.at[i]) for i, (a, b) in enumerate(zip(sources, targets))]
    for copy in copies:
        copy.start()
    bins, _ = x_ref.shape
    tiles = [slice(b * TILE, (b + 1) * TILE) for b in range(bins // TILE)]
    copies[0].wait()
    copies[1].wait()
    for bs in tiles:
        do = mm(up_ref[bs, :], wo_ref[...], 1, 1).astype(BF16)
        do_ref[bs, :] = do
        dot_ref[:, bs] = do.T
    copies[2].wait()
    copies[3].wait()
    for bs in tiles:
        q = (mm(x_ref[bs, :], wq_ref[...], 1, 0) * (SCALE * LOG2E)).astype(BF16)
        q_ref[bs, :] = q
        qt_ref[:, bs] = q.T
        xt_ref[:, bs] = x_ref[bs, :].T
    copies[4].wait()
    copies[5].wait()
    for bs in tiles:
        k = mm(x_ref[bs, :], wk_ref[...], 1, 0).astype(BF16)
        k_ref[bs, :] = k
        kt_ref[:, bs] = k.T
        v_ref[bs, :] = mm(x_ref[bs, :], wv_ref[...], 1, 0).astype(BF16)
    copies[6].wait()
    copies[7].wait()
    lane = lax.broadcasted_iota(jnp.int32, (1, 128), 1)
    for bs in tiles:
        prod = do_ref[bs, :].astype(F32) * saved_ref[bs, :].astype(F32)
        padded = jnp.concatenate([lse_ref[:, bs] * LOG2E, jnp.zeros((128 - HEADS, TILE), F32)], axis=0)
        aux = padded.T
        for head in range(HEADS):
            slab = prod[:, head // 2 * 128 : head // 2 * 128 + 128]
            off = jnp.sum(jnp.where(half_mask(head % 2), slab, 0.0), axis=1, keepdims=True)
            aux = jnp.where(lane == HEADS + head, off, aux)
        aux_ref[bs, :] = aux
    gwo_ref[...] = mm(saved_ref[...], up_ref[...], 0, 0)

    def put_query(rows, qs, value):
        dqt_ref[rows, qs] = value

    def put_key(rows, ks, value):
        dkt_ref[rows, ks] = value.astype(BF16)

    def put_value(rows, ks, value):
        dvt_ref[rows, ks] = value.astype(BF16)

    attention(
        True, (q_ref, do_ref, qt_ref, dot_ref, k_ref, v_ref, kt_ref, aux_ref), scratch, put_query, put_key, put_value
    )


def far_kernel(
    xp_ref, wk_ref, wv_ref, q_ref, do_ref, qt_ref, dot_ref, aux_ref, dqn_ref,
    dqt_ref, dkf, dvf, xpt,
    k_ref, v_ref, kt_ref, *scratch,
):
    bins, _ = xp_ref.shape
    for b in range(bins // TILE):
        bs = slice(b * TILE, (b + 1) * TILE)
        xp = xp_ref[bs, :]
        k = mm(xp, wk_ref[...], 1, 0).astype(BF16)
        k_ref[bs, :] = k
        kt_ref[:, bs] = k.T
        v_ref[bs, :] = mm(xp, wv_ref[...], 1, 0).astype(BF16)
        xpt[:, bs] = xp.T

    def put_query(rows, qs, value):
        dqt_ref[rows, qs] = (dqn_ref[rows, qs] + value).astype(BF16)

    def put_key(rows, ks, value):
        dkf[rows, ks] = value.astype(BF16)

    def put_value(rows, ks, value):
        dvf[rows, ks] = value.astype(BF16)

    attention(
        False, (q_ref, do_ref, qt_ref, dot_ref, k_ref, v_ref, kt_ref, aux_ref), scratch, put_query, put_key, put_value
    )


def back_kernel(dkf_ref, dvf_ref, wk_ref, wv_ref, out_ref):
    out_ref[...] = (mm(wk_ref[...], dkf_ref[...], 1, 0) + mm(wv_ref[...], dvf_ref[...], 1, 0)).astype(BF16)


def bit_order(bits, parity):
    rest = list(range(1, bits))
    turn = (2, 1, 0) if parity == 0 else (1, 2, 0)
    return [rest[t] for t in turn] + rest[3:] if len(rest) >= 3 else rest


def place(device, order):
    return sum(((device >> bit) & 1) << (len(order) - 1 - t) for t, bit in enumerate(order))


def weight_kernel(count, xt_ref, xpt_ref, dqt_ref, dkt_ref, dvt_ref, dkf_ref, dvf_ref, gwo_ref, send_ref, both_ref):
    width = xt_ref.shape[0]
    rows = 4 * width // count
    bits = count.bit_length() - 1

    def put(which, value):
        for block in range(width // rows):
            device = which * (width // rows) + block
            at = place(device, bit_order(bits, device & 1))
            both_ref[device & 1, at * rows : (at + 1) * rows, :] = value[block * rows : (block + 1) * rows, :]

    put(0, mm(xt_ref[...], dqt_ref[...], 1, 1))
    put(1, mm(xt_ref[...], dkt_ref[...], 1, 1) + mm(xpt_ref[...], dkf_ref[...], 1, 1))
    put(2, mm(xt_ref[...], dvt_ref[...], 1, 1) + mm(xpt_ref[...], dvf_ref[...], 1, 1))
    put(3, gwo_ref[...])
    send_ref[...] = both_ref[1 - lax.axis_index(("dp", "tm")) % 2].astype(BF16)


def halve_kernel(even_bit, odd_bit, keep_ref, got_ref, send_ref, out_ref):
    half = out_ref.shape[0]
    me = lax.axis_index(("dp", "tm"))
    bit = jnp.where(me % 2 == 1, me >> odd_bit, me >> even_bit) & 1
    mine = pl.ds(pl.multiple_of(bit * half, half), half)
    other = pl.ds(pl.multiple_of((1 - bit) * half, half), half)
    kept = keep_ref.at[me % 2] if len(keep_ref.shape) == 3 else keep_ref
    send_ref[...] = (kept[other, :] + got_ref[other, :].astype(F32)).astype(BF16)
    out_ref[...] = kept[mine, :] + got_ref[mine, :].astype(F32)


def add_kernel(keep_ref, got_ref, out_ref):
    out_ref[...] = keep_ref[...] + got_ref[...].astype(F32)


def near_input_kernel(dq_ref, dkt_ref, dvt_ref, wq_ref, wk_ref, wv_ref, out_ref):
    out_ref[...] = (
        mm(wq_ref[...], dq_ref[...], 1, 0) + mm(wk_ref[...], dkt_ref[...], 1, 0) + mm(wv_ref[...], dvt_ref[...], 1, 0)
    )


def input_kernel(near_ref, back_ref, out_ref):
    bins = out_ref.shape[0]
    for b in range(bins // TILE):
        bs = slice(b * TILE, (b + 1) * TILE)
        out_ref[bs, :] = (near_ref[:, bs] + back_ref[:, bs].astype(F32)).T.astype(BF16)


def call(kernel, outs, scratch, flops, *args, specs=None, limit=28):
    return pl.pallas_call(
        kernel,
        out_shape=outs,
        in_specs=specs or [VMEM] * len(args),
        out_specs=[VMEM] * len(outs),
        scratch_shapes=scratch,
        compiler_params=pltpu.CompilerParams(vmem_limit_bytes=limit * 2**20),
        cost_estimate=pl.CostEstimate(
            flops=int(flops), bytes_accessed=sum(a.size * a.dtype.itemsize for a in args), transcendentals=0
        ),
    )(*args)


def on_chip(x):
    return pltpu.with_memory_space_constraint(x, pltpu.VMEM)


def scatter_sum(send, keep, axes):
    count = lax.axis_size(axes)
    bits = count.bit_length() - 1
    width = keep.shape[-1]
    got = lax.ppermute(send, axes, [(d, d ^ 1) for d in range(count)])
    for even_bit, odd_bit in zip(bit_order(bits, 0), bit_order(bits, 1)):
        half = keep.shape[-2] // 2
        send, keep = call(
            functools.partial(halve_kernel, even_bit, odd_bit),
            [pltpu.VMEM((half, width), BF16), pltpu.VMEM((half, width), F32)],
            [],
            keep.size,
            on_chip(keep),
            on_chip(got),
        )
        steps = (1 << even_bit, 1 << odd_bit)
        got = lax.ppermute(send, axes, [(d, d ^ steps[d & 1]) for d in range(count)])
    (out,) = call(add_kernel, [jax.ShapeDtypeStruct(keep.shape, F32)], [], keep.size, on_chip(keep), on_chip(got))
    return out


def on_device(inputs, w_query, w_key, w_value, w_out, saved_heads, log_totals, out_grad):
    x, saved, lse, up = inputs[0], saved_heads[0], log_totals[0], out_grad[0]
    bins, width = x.shape
    tm = lax.axis_size("tm")
    axes = ("dp", "tm")
    count = lax.axis_size(axes)
    x_prev = lax.ppermute(x, "tm", [(s, s + 1) for s in range(tm - 1)])
    tall, wide, square = (bins, width), (width, bins), (width, width)
    one = 2 * bins * width * width
    band = 2 * HEADS * bins * bins * HEAD_DIM * 5
    q, do, qt, dot, aux, dqn, dkt, dvt, gwo, xt, wq, wk, wv = call(
        near_kernel,
        [pltpu.VMEM(s, d) for s, d in (
            (tall, BF16), (tall, BF16), (wide, BF16), (wide, BF16), ((bins, 128), F32), (wide, F32), (wide, BF16),
            (wide, BF16), (square, F32), (wide, BF16), (square, BF16), (square, BF16), (square, BF16),
        )],
        [pltpu.VMEM(s, d) for s, d in (
            (tall, BF16), (square, BF16), (tall, BF16), (tall, BF16), ((HEADS, bins), F32), (tall, BF16), (tall, BF16), (wide, BF16),
        )] + [pltpu.SemaphoreType.DMA((8,))] + attention_scratch(bins),
        band,
        *[pltpu.with_memory_space_constraint(a, pltpu.HBM) for a in (x, w_query, w_key, w_value, w_out, saved, up, lse)],
        specs=[pl.BlockSpec(memory_space=pltpu.HBM)] * 8,
    )
    dq, dkf, dvf, xpt = call(
        far_kernel,
        [pltpu.VMEM(wide, BF16)] * 4,
        [pltpu.VMEM(s, BF16) for s in (tall, tall, wide)] + attention_scratch(bins),
        band,
        on_chip(x_prev), wk, wv, q, do, qt, dot, aux, dqn,
    )
    half = (2 * width, width)
    send, keep = call(
        functools.partial(weight_kernel, count),
        [pltpu.VMEM(half, BF16), pltpu.VMEM((2, *half), F32)],
        [],
        5 * one,
        xt, xpt, dq, dkt, dvt, dkf, dvf, gwo,
    )
    (back,) = call(back_kernel, [pltpu.VMEM(wide, BF16)], [], 2 * one, dkf, dvf, wk, wv)
    back = lax.ppermute(back, "tm", [(s + 1, s) for s in range(tm - 1)])
    weight_grads = scatter_sum(send, keep, axes)
    (near_grad,) = call(near_input_kernel, [pltpu.VMEM(wide, F32)], [], 3 * one, dq, dkt, dvt, wq, wk, wv)
    (input_grad,) = call(input_kernel, [jax.ShapeDtypeStruct(tall, BF16)], [], one // 8, near_grad, on_chip(back))
    return input_grad[None], weight_grads


def solution(mesh):
    rows, copied = P("dp", "tm", None), P()

    return jax.shard_map(
        on_device,
        mesh=mesh,
        in_specs=(rows, copied, copied, copied, copied, rows, P("dp", None, "tm"), rows),
        out_specs=(rows, P(("dp", "tm"), None)),
        check_vma=False,
    )
```

```python
import functools
import math

import jax
import jax.numpy as jnp
from jax import lax
from jax.experimental import pallas as pl
from jax.experimental.pallas import tpu as pltpu
from jax.sharding import PartitionSpec as P


HEADS = 8
HEAD_DIM = 64
TILE = 256
SCALE = HEAD_DIM**-0.5
LOG2E = math.log2(math.e)
LN2 = math.log(2.0)
F32 = jnp.float32
BF16 = jnp.bfloat16
VMEM = pl.BlockSpec(memory_space=pltpu.VMEM)


def mm(a, b, ca, cb):
    return lax.dot_general(a, b, (((ca,), (cb,)), ((), ())), preferred_element_type=F32)


def twice(x):
    return jnp.concatenate([x, x], axis=1)


def half_mask(h):
    lane = lax.broadcasted_iota(jnp.int32, (1, 128), 1)
    return lane < HEAD_DIM if h == 0 else lane >= HEAD_DIM


def attention(near, refs, scratch, put_query, put_key, put_value):
    q_ref, do_ref, saved_ref, qt_ref, dot_ref, k_ref, v_ref, kt_ref, aux_ref = refs
    km, vm, lseb, offb, prob, grad, grad_t = scratch
    bins = q_ref.shape[0]
    blocks = bins // TILE

    def body(pair, carry):
        base = pl.multiple_of(pair * 128, 128)
        cols = pl.ds(base, 128)
        for h in range(2):
            rows = pl.ds(pl.multiple_of(base + h * HEAD_DIM, HEAD_DIM), HEAD_DIM)
            mask = half_mask(h)
            k2, v2 = k_ref[:, cols], v_ref[:, cols]
            km[h] = jnp.where(mask, k2, jnp.zeros_like(k2))
            vm[h] = jnp.where(mask, v2, jnp.zeros_like(v2))
            lane = lax.broadcasted_iota(jnp.int32, (1, 128), 1)
            aux = aux_ref[...]
            head = pair * 2 + h
            lse = jnp.sum(jnp.where(lane == head, aux, 0.0), axis=1, keepdims=True)
            prod = do_ref[:, cols].astype(F32) * saved_ref[:, cols].astype(F32)
            off = jnp.sum(jnp.where(mask, prod, 0.0), axis=1, keepdims=True)
            lseb[...] = jnp.broadcast_to(lse, (bins, 128))
            offb[...] = jnp.broadcast_to(off, (bins, 128))
            for j in range(blocks):
                ks = slice(j * TILE, (j + 1) * TILE)
                kw, vw = km[h, ks, :], vm[h, ks, :]
                for i in range(j, blocks) if near else range(j + 1):
                    qs = slice(i * TILE, (i + 1) * TILE)
                    p = jnp.exp2(mm(q_ref[qs, cols], kw, 1, 1) - twice(lseb[qs, :]))
                    if i == j:
                        r = lax.broadcasted_iota(jnp.int32, (TILE, TILE), 0)
                        c = lax.broadcasted_iota(jnp.int32, (TILE, TILE), 1)
                        p = jnp.where(r >= c if near else r < c, p, 0.0)
                    dp = mm(do_ref[qs, cols], vw, 1, 1)
                    prob[h, qs, ks] = p.astype(BF16)
                    g = (p * (dp - twice(offb[qs, :]))).astype(BF16)
                    grad[h, qs, ks] = g
                    grad_t[h, ks, qs] = g.T
            for j in range(blocks):
                ks = slice(j * TILE, (j + 1) * TILE)
                qs = slice(j * TILE, bins) if near else slice(0, (j + 1) * TILE)
                put_value(rows, ks, mm(dot_ref[rows, qs], prob[h, qs, ks], 1, 0))
                put_key(rows, ks, mm(qt_ref[rows, qs], grad[h, qs, ks], 1, 0) * LN2)
            for i in range(blocks):
                qs = slice(i * TILE, (i + 1) * TILE)
                ks = slice(0, (i + 1) * TILE) if near else slice(i * TILE, bins)
                put_query(rows, qs, mm(kt_ref[rows, ks], grad_t[h, ks, qs], 1, 0) * SCALE)
        return carry

    lax.fori_loop(0, HEADS // 2, body, 0)


def attention_scratch(bins):
    return [
        pltpu.VMEM((2, bins, 128), BF16),
        pltpu.VMEM((2, bins, 128), BF16),
        pltpu.VMEM((bins, 128), F32),
        pltpu.VMEM((bins, 128), F32),
        pltpu.VMEM((2, bins, bins), BF16),
        pltpu.VMEM((2, bins, bins), BF16),
        pltpu.VMEM((2, bins, bins), BF16),
    ]


def near_kernel(
    x_hbm, wq_hbm, wk_hbm, wv_hbm, wo_hbm, saved_hbm, up_hbm, lse_hbm,
    q_ref, do_ref, qt_ref, dot_ref, aux_ref, dqt_ref, dkt_ref, dvt_ref, gwo_ref, x_ref, saved_ref, wq_ref, wk_ref, wv_ref,
    wo_ref, up_ref, lse_ref, k_ref, v_ref, kt_ref, sems, *scratch,
):
    sources = (up_hbm, wo_hbm, x_hbm, wq_hbm, wk_hbm, wv_hbm, saved_hbm, lse_hbm)
    targets = (up_ref, wo_ref, x_ref, wq_ref, wk_ref, wv_ref, saved_ref, lse_ref)
    copies = [pltpu.make_async_copy(a, b, sems.at[i]) for i, (a, b) in enumerate(zip(sources, targets))]
    for copy in copies:
        copy.start()
    for copy in copies:
        copy.wait()
    bins, _ = x_ref.shape
    tiles = [slice(b * TILE, (b + 1) * TILE) for b in range(bins // TILE)]
    for bs in tiles:
        do = mm(up_ref[bs, :], wo_ref[...], 1, 1).astype(BF16)
        do_ref[bs, :] = do
        dot_ref[:, bs] = do.T
    for bs in tiles:
        q = (mm(x_ref[bs, :], wq_ref[...], 1, 0) * (SCALE * LOG2E)).astype(BF16)
        q_ref[bs, :] = q
        qt_ref[:, bs] = q.T
    for bs in tiles:
        k = mm(x_ref[bs, :], wk_ref[...], 1, 0).astype(BF16)
        k_ref[bs, :] = k
        kt_ref[:, bs] = k.T
        v_ref[bs, :] = mm(x_ref[bs, :], wv_ref[...], 1, 0).astype(BF16)
    for bs in tiles:
        padded = jnp.concatenate([lse_ref[:, bs] * LOG2E, jnp.zeros((128 - HEADS, TILE), F32)], axis=0)
        aux_ref[bs, :] = padded.T
    gwo_ref[...] = mm(saved_ref[...], up_ref[...], 0, 0)

    def put_query(rows, qs, value):
        dqt_ref[rows, qs] = value

    def put_key(rows, ks, value):
        dkt_ref[rows, ks] = value.astype(BF16)

    def put_value(rows, ks, value):
        dvt_ref[rows, ks] = value.astype(BF16)

    attention(
        True, (q_ref, do_ref, saved_ref, qt_ref, dot_ref, k_ref, v_ref, kt_ref, aux_ref), scratch, put_query, put_key, put_value
    )


def far_kernel(
    xp_ref, wk_ref, wv_ref, q_ref, do_ref, saved_ref, qt_ref, dot_ref, aux_ref, dqn_ref,
    dqt_ref, dkf, dvf,
    k_ref, v_ref, kt_ref, *scratch,
):
    bins, _ = xp_ref.shape
    for b in range(bins // TILE):
        bs = slice(b * TILE, (b + 1) * TILE)
        xp = xp_ref[bs, :]
        k = mm(xp, wk_ref[...], 1, 0).astype(BF16)
        k_ref[bs, :] = k
        kt_ref[:, bs] = k.T
        v_ref[bs, :] = mm(xp, wv_ref[...], 1, 0).astype(BF16)

    def put_query(rows, qs, value):
        dqt_ref[rows, qs] = (dqn_ref[rows, qs] + value).astype(BF16)

    def put_key(rows, ks, value):
        dkf[rows, ks] = value.astype(BF16)

    def put_value(rows, ks, value):
        dvf[rows, ks] = value.astype(BF16)

    attention(
        False, (q_ref, do_ref, saved_ref, qt_ref, dot_ref, k_ref, v_ref, kt_ref, aux_ref), scratch, put_query, put_key, put_value
    )


def back_kernel(dkf_ref, dvf_ref, wk_ref, wv_ref, out_ref):
    out_ref[...] = (mm(wk_ref[...], dkf_ref[...], 1, 0) + mm(wv_ref[...], dvf_ref[...], 1, 0)).astype(BF16)


def bit_order(bits, parity):
    rest = list(range(1, bits))
    turn = (2, 1, 0, 3) if parity == 0 else (1, 2, 3, 0)
    return [rest[t] for t in turn] + rest[4:] if len(rest) >= 4 else rest


def place(device, order):
    return sum(((device >> bit) & 1) << (len(order) - 1 - t) for t, bit in enumerate(order))


def weight_kernel(count, x_ref, xp_ref, dqt_ref, dkt_ref, dvt_ref, dkf_ref, dvf_ref, gwo_ref, send_ref, keep_ref):
    width = x_ref.shape[1]
    rows = 4 * width // count
    bits = count.bit_length() - 1
    products = (
        lambda: mm(dqt_ref[...], x_ref[...], 1, 0).T,
        lambda: (mm(dkt_ref[...], x_ref[...], 1, 0) + mm(dkf_ref[...], xp_ref[...], 1, 0)).T,
        lambda: (mm(dvt_ref[...], x_ref[...], 1, 0) + mm(dvf_ref[...], xp_ref[...], 1, 0)).T,
        lambda: gwo_ref[...],
    )
    mine = lax.axis_index(("dp", "tm")) % 2
    for parity in range(2):

        @pl.when(mine == parity)
        def _(parity=parity):
            for which, product in enumerate(products):
                value = product()
                for block in range(width // rows):
                    device = which * (width // rows) + block
                    at = place(device, bit_order(bits, device & 1))
                    piece = value[block * rows : (block + 1) * rows, :]
                    if device & 1 == parity:
                        keep_ref[at * rows : (at + 1) * rows, :] = piece
                    else:
                        send_ref[at * rows : (at + 1) * rows, :] = piece.astype(BF16)


def halve_kernel(even_bit, odd_bit, keep_ref, got_ref, send_ref, out_ref):
    half = out_ref.shape[0]
    me = lax.axis_index(("dp", "tm"))
    bit = jnp.where(me % 2 == 1, me >> odd_bit, me >> even_bit) & 1
    mine = pl.ds(pl.multiple_of(bit * half, half), half)
    other = pl.ds(pl.multiple_of((1 - bit) * half, half), half)
    send_ref[...] = (keep_ref[other, :] + got_ref[other, :].astype(F32)).astype(BF16)
    out_ref[...] = keep_ref[mine, :] + got_ref[mine, :].astype(F32)


def add_kernel(keep_ref, got_ref, out_ref):
    out_ref[...] = keep_ref[...] + got_ref[...].astype(F32)


def near_input_kernel(dq_ref, dkt_ref, dvt_ref, wq_ref, wk_ref, wv_ref, out_ref):
    out_ref[...] = (
        mm(wq_ref[...], dq_ref[...], 1, 0) + mm(wk_ref[...], dkt_ref[...], 1, 0) + mm(wv_ref[...], dvt_ref[...], 1, 0)
    )


def input_kernel(near_ref, back_ref, out_ref):
    bins = out_ref.shape[0]
    for b in range(bins // TILE):
        bs = slice(b * TILE, (b + 1) * TILE)
        out_ref[bs, :] = (near_ref[:, bs] + back_ref[:, bs].astype(F32)).T.astype(BF16)


def call(kernel, outs, scratch, flops, *args, specs=None, limit=28):
    return pl.pallas_call(
        kernel,
        out_shape=outs,
        in_specs=specs or [VMEM] * len(args),
        out_specs=[VMEM] * len(outs),
        scratch_shapes=scratch,
        compiler_params=pltpu.CompilerParams(vmem_limit_bytes=limit * 2**20),
        cost_estimate=pl.CostEstimate(
            flops=int(flops), bytes_accessed=sum(a.size * a.dtype.itemsize for a in args), transcendentals=0
        ),
    )(*args)


def on_chip(x):
    return pltpu.with_memory_space_constraint(x, pltpu.VMEM)


def scatter_sum(send, keep, axes):
    count = lax.axis_size(axes)
    bits = count.bit_length() - 1
    width = keep.shape[-1]
    got = lax.ppermute(send, axes, [(d, d ^ 1) for d in range(count)])
    for even_bit, odd_bit in zip(bit_order(bits, 0), bit_order(bits, 1)):
        half = keep.shape[-2] // 2
        send, keep = call(
            functools.partial(halve_kernel, even_bit, odd_bit),
            [pltpu.VMEM((half, width), BF16), pltpu.VMEM((half, width), F32)],
            [],
            keep.size,
            on_chip(keep),
            on_chip(got),
        )
        steps = (1 << even_bit, 1 << odd_bit)
        got = lax.ppermute(send, axes, [(d, d ^ steps[d & 1]) for d in range(count)])
    (out,) = call(add_kernel, [jax.ShapeDtypeStruct(keep.shape, F32)], [], keep.size, on_chip(keep), on_chip(got))
    return out


def on_device(inputs, w_query, w_key, w_value, w_out, saved_heads, log_totals, out_grad):
    x, saved, lse, up = inputs[0], saved_heads[0], log_totals[0], out_grad[0]
    bins, width = x.shape
    tm = lax.axis_size("tm")
    axes = ("dp", "tm")
    count = lax.axis_size(axes)
    x_prev = lax.ppermute(x, "tm", [(s, s + 1) for s in range(tm - 1)])
    tall, wide, square = (bins, width), (width, bins), (width, width)
    one = 2 * bins * width * width
    band = 2 * HEADS * bins * bins * HEAD_DIM * 5
    q, do, qt, dot, aux, dqn, dkt, dvt, gwo, x_own, saved_own, wq, wk, wv = call(
        near_kernel,
        [pltpu.VMEM(s, d) for s, d in (
            (tall, BF16), (tall, BF16), (wide, BF16), (wide, BF16), ((bins, 128), F32), (wide, F32), (wide, BF16),
            (wide, BF16), (square, F32), (tall, BF16), (tall, BF16), (square, BF16), (square, BF16), (square, BF16),
        )],
        [pltpu.VMEM(s, d) for s, d in (
            (square, BF16), (tall, BF16), ((HEADS, bins), F32), (tall, BF16), (tall, BF16), (wide, BF16),
        )] + [pltpu.SemaphoreType.DMA((8,))] + attention_scratch(bins),
        band,
        *[pltpu.with_memory_space_constraint(a, pltpu.HBM) for a in (x, w_query, w_key, w_value, w_out, saved, up, lse)],
        specs=[pl.BlockSpec(memory_space=pltpu.HBM)] * 8,
    )
    x_prev = on_chip(x_prev)
    dq, dkf, dvf = call(
        far_kernel,
        [pltpu.VMEM(wide, BF16)] * 3,
        [pltpu.VMEM(s, BF16) for s in (tall, tall, wide)] + attention_scratch(bins),
        band,
        x_prev, wk, wv, q, do, saved_own, qt, dot, aux, dqn,
    )
    half = (2 * width, width)
    send, keep = call(
        functools.partial(weight_kernel, count),
        [pltpu.VMEM(half, BF16), pltpu.VMEM(half, F32)],
        [],
        5 * one,
        x_own, x_prev, dq, dkt, dvt, dkf, dvf, gwo,
    )
    (back,) = call(back_kernel, [pltpu.VMEM(wide, BF16)], [], 2 * one, dkf, dvf, wk, wv)
    back = lax.ppermute(back, "tm", [(s + 1, s) for s in range(tm - 1)])
    weight_grads = scatter_sum(send, keep, axes)
    (near_grad,) = call(near_input_kernel, [pltpu.VMEM(wide, F32)], [], 3 * one, dq, dkt, dvt, wq, wk, wv)
    (input_grad,) = call(input_kernel, [jax.ShapeDtypeStruct(tall, BF16)], [], one // 8, near_grad, on_chip(back))
    return input_grad[None], weight_grads


def solution(mesh):
    rows, copied = P("dp", "tm", None), P()

    return jax.shard_map(
        on_device,
        mesh=mesh,
        in_specs=(rows, copied, copied, copied, copied, rows, P("dp", None, "tm"), rows),
        out_specs=(rows, P(("dp", "tm"), None)),
        check_vma=False,
    )
```
